256 devices in a mesh: grp: 16 (over z_lo, x, core), peak: 16 (over y, z_hi).
Axes of the slice: x: 4, y: 4, z: 8 (z_hi: 4, z_lo: 2; z = z_hi * 2 + z_lo), core: 2. Of those that a mesh axis runs over, the one named last changes fastest.
Arguments:
- counts: bfloat16 [1024, 524288], P(None, ('grp', 'peak')), may hold values from 0.099609375 to 4
- tile_mask: int32 [1024, 4096], P(None, ('grp', 'peak')), may hold values 0 or 1
- neighbours: int32 [1024, 15], P(('grp', 'peak')), may hold values from 0 to 1023, as said below
- peak_weight: bfloat16 [524288, 512], P(('grp', 'peak')), may hold values from -0.013671875 to 0.013671875
- gain: float32 [512], replicated, may hold values from 0.25 to 1.75
- w_in: bfloat16 [512, 512], replicated, may hold values from -0.25 to 0.25
- w_out: bfloat16 [512, 256], replicated, may hold values from -0.25 to 0.25
Outputs:
- peak_grad: float32 [524288, 512], P(('grp', 'peak'))
- gain_grad: float32 [512], replicated
- in_grad: float32 [512, 512], replicated
- out_grad: float32 [512, 256], replicated
The draws below stay inside these ranges and needn't reach their ends.
Inputs may be any that keep to these rules, and one draw needn't show every extreme that they name: `neighbours`: every entry is a cell index other than its own row's cell.
All inputs are finite; a program needn't handle non-finite values. No bound on the sum of `tile_mask` on one device may be relied on, other than what follows from the above.
Results may differ from the reference program's by a relative error of at most 0.012.
Values may be sent and summed in bfloat16 or wider, within the bound.
A program may use at most 64 MiB of HBM per device.

```python
import math
import jax
import jax.numpy as jnp
from jax import lax

D = 512
HID = 512
E = 256
TILE = 128
K = 15
CELLS = 1024
PEAKS = 524288
TILES = 4096


def draw_neighbours(key, part):
    offsets = jax.random.randint(key, (CELLS, K), 1, CELLS)
    base_rows = jnp.arange(CELLS, dtype=jnp.int32)[:, None]
    return ((base_rows + offsets) % CELLS).astype(jnp.int32)


def set_ends(values, key, smallest, top_value):
    longest = values.shape.index(max(values.shape))
    spots = []
    for shift in (0, 1):
        where = [jax.random.randint(jax.random.fold_in(key, axis), (), 0, length) for axis, length in enumerate(values.shape)]
        where[longest] = (where[longest] + shift) % values.shape[longest]
        spots.append(tuple(where))
    return values.at[spots[0]].set(smallest).at[spots[1]].set(top_value)


def levels(stream_key, shape, shards, smallest, largest):
    level = 1.0
    for dim, shards_of in shards:
        heights = jax.random.uniform(jax.random.fold_in(jax.random.fold_in(stream_key, 6), dim), (shards_of,), jnp.float32, smallest / len(shards), largest / len(shards))
        level = level * jnp.repeat(jnp.exp(heights), shape[dim] // shards_of).reshape((-1,) + (1,) * (len(shape) - 1 - dim))
    return level


def scatter_about(key, extent, spread, bound, split=(), kind=jnp.bfloat16):
    factor_of = levels(key, extent, split, -0.22, 0.18) if split else 1.0
    entries = jax.random.normal(key, extent, jnp.float32) * spread * factor_of
    return jnp.minimum(jnp.maximum(entries, -bound), bound).astype(kind)


def setup_inputs(seed: int = 0) -> dict:
    key_list = jax.random.split(jax.random.key(seed), 8)
    return {
        "counts": jnp.clip(jnp.exp(math.log(4.0) - 3.6927934 * jax.random.uniform(key_list[0], (CELLS, PEAKS), jnp.float32) ** levels(key_list[0], (CELLS, PEAKS), ((1, 256),), -0.2, 0.2)), 0.099609375, 4.0).astype(jnp.bfloat16),
        "tile_mask": set_ends((jax.random.randint(key_list[1], (CELLS, TILES), 0, 3) < 1).astype(jnp.int32), jax.random.fold_in(key_list[1], 1), 0, 1),
        "neighbours": draw_neighbours(jax.random.fold_in(key_list[7], 71), 0),
        "peak_weight": scatter_about(key_list[3], (PEAKS, D), (PEAKS // 3) ** -0.5, 0.013671875, ((0, 256),)),
        "gain": jnp.clip(1.0 + 0.15 * jax.random.normal(key_list[4], (D,), jnp.float32), 0.25, 1.75),
        "w_in": scatter_about(key_list[5], (D, HID), D ** -0.5, 0.25),
        "w_out": scatter_about(key_list[6], (HID, E), HID ** -0.5, 0.25),
    }


sharpness_divisor = 0.2
eps_norm = 1e-06
gelu_coef = 0.7978845608
cubic_coef = 0.044715

def gelu_tanh(values):
    return 0.5 * values * (1.0 + jnp.tanh(gelu_coef * (values + cubic_coef * values * values * values)))

def gelu_slope(values):
    tangent = jnp.tanh(gelu_coef * (values + cubic_coef * values * values * values))
    return 0.5 * (1.0 + tangent) + 0.5 * values * (1.0 - tangent * tangent) * gelu_coef * (1.0 + 3.0 * cubic_coef * values * values)

def collapsed_lines(left, right):
    return lax.dot_general(left, right, (((0,), (0,)), ((), ())), preferred_element_type=jnp.float32)

def tower_forward(hidden, gain, w_in, w_out):
    scale = lax.rsqrt(lax.optimization_barrier(jnp.mean(hidden * hidden, axis=1, keepdims=True)) + eps_norm)
    normed = hidden * scale
    rounded = (normed * gain[None, :]).astype(jnp.bfloat16)
    preact = jnp.dot(rounded, w_in, preferred_element_type=jnp.float32)
    activ = gelu_tanh(preact).astype(jnp.bfloat16)
    project = jnp.dot(activ, w_out, preferred_element_type=jnp.float32)
    length = lax.rsqrt(lax.optimization_barrier(jnp.sum(project * project, axis=1, keepdims=True)) + eps_norm)
    unit = project * length
    return ((scale, normed, rounded, preact, activ, length, unit), unit.astype(jnp.bfloat16))

def tower_backward(vector_derivative, gain, w_in, w_out, saved):
    scale, normed, rounded, preact, activ, length, unit = saved
    dproj = (length * (vector_derivative - unit * lax.optimization_barrier(jnp.sum(unit * vector_derivative, axis=1, keepdims=True)))).astype(jnp.bfloat16)
    out_grad = collapsed_lines(activ, dproj)
    dact = jnp.dot(dproj, w_out.T, preferred_element_type=jnp.float32)
    dpre = (dact * gelu_slope(preact)).astype(jnp.bfloat16)
    in_grad = collapsed_lines(rounded, dpre)
    dround = jnp.dot(dpre, w_in.T, preferred_element_type=jnp.float32)
    gain_grad = lax.optimization_barrier(jnp.sum(dround * normed, axis=0))
    dnorm = dround * gain[None, :]
    dhidden = scale * (dnorm - normed * lax.optimization_barrier(jnp.mean(dnorm * normed, axis=1, keepdims=True)))
    return (dhidden.astype(jnp.bfloat16), gain_grad, in_grad, out_grad)

def reference(counts, tile_mask, neighbours, peak_weight, gain, w_in, w_out):
    masked = counts * jnp.repeat(tile_mask.astype(jnp.bfloat16), TILE, axis=1)
    hidden = jnp.dot(masked, peak_weight, preferred_element_type=jnp.float32)
    saved, sample_vectors = tower_forward(hidden, gain, w_in, w_out)
    affinity_scores = jnp.dot(sample_vectors, sample_vectors.T, preferred_element_type=jnp.float32) / sharpness_divisor
    rows = lax.broadcasted_iota(jnp.int32, (CELLS, CELLS), 0)
    cols = lax.broadcasted_iota(jnp.int32, (CELLS, CELLS), 1)
    expo = jnp.where(rows == cols, jnp.float32(0.0), jnp.exp(affinity_scores))
    prob = expo / lax.optimization_barrier(jnp.sum(expo, axis=1, keepdims=True))
    tallies = jnp.zeros((CELLS, CELLS), jnp.float32)
    for slot in range(K):
        tallies = tallies + (neighbours[:, slot][:, None] == cols).astype(jnp.float32)
    neighbour_coefficients = (prob - tallies / K).astype(jnp.bfloat16)
    vector_derivative = (jnp.dot(neighbour_coefficients, sample_vectors, preferred_element_type=jnp.float32) + collapsed_lines(neighbour_coefficients, sample_vectors)) / sharpness_divisor
    dhidden, gain_grad, in_grad, out_grad = tower_backward(vector_derivative, gain, w_in, w_out, saved)
    peak_grad = collapsed_lines(masked, dhidden)
    return (peak_grad, gain_grad, in_grad, out_grad)
```

```python
import jax
import jax.numpy as jnp
from jax import lax
from jax.experimental import pallas as pl
from jax.experimental.pallas import tpu as pltpu
from jax.sharding import PartitionSpec as P

TILE = 128
K = 15
CELLS = 1024
D = 512
HID = 512
E = 256
LOCAL = 2048
HALF = CELLS // 2
PIECE = HALF // 16
BLOCK = 256
SLOT = 16

sharpness = 5.0
eps_norm = 1e-06
gelu_coef = 0.7978845608
cubic_coef = 0.044715

bf16 = jnp.bfloat16
f32 = jnp.float32
i32 = jnp.int32
MESH = pl.DeviceIdType.MESH


def coordinates():
    grp = lax.axis_index("grp")
    peak = lax.axis_index("peak")
    return (grp // 2) % 4, peak // 4, (peak % 4) * 2 + grp // 8, grp % 2


def device(x, y, z, core):
    return {"grp": ((z % 2) * 4 + x) * 2 + core, "peak": y * 4 + z // 2}


def rows_of(start, size):
    return pl.ds(pl.multiple_of(start, size), size)


def gather_kernel(
    counts, tile_mask, neighbours, weight,
    hidden_out, turned_out, tallies_out,
    loaded, masked, turned, w_buf, partial, core_send, core_recv, plane_send, plane_recv,
    column, hidden, lists, list_rows, counted, tallies,
    load_sem, w_sem, core_ss, core_rs, plane_ss, plane_rs, z_ss, z_rs,
    out_ss, out_rs, fwd_ss, fwd_rs, list_ss, list_rs, store_sem,
):
    x, y, z, core = coordinates()
    plane = x * 4 + y
    sibling = device(x, y, z, 1 - core)

    def plane_at(step):
        return (x + step // 4) % 4, (y + step % 4) % 4

    def plane_from(step):
        return (x + 4 - step // 4) % 4, (y + 4 - step % 4) % 4

    barrier = pltpu.get_barrier_semaphore()
    pl.semaphore_signal(barrier, inc=1, device_id=sibling, device_id_type=MESH)

    def greet_plane(step, carry):
        px, py = plane_at(step)
        pl.semaphore_signal(barrier, inc=1, device_id=device(px, py, z, core), device_id_type=MESH)
        return carry

    def greet_column(step, carry):
        pl.semaphore_signal(
            barrier, inc=1, device_id=device(x, y, (z + step) % 8, core), device_id_type=MESH
        )
        return carry

    lax.fori_loop(1, 16, greet_plane, 0)
    lax.fori_loop(1, 8, greet_column, 0)

    def block_start(step):
        return HALF * ((1 - core + step // 2) % 2) + BLOCK * (step % 2)

    def load(step):
        rows = rows_of(block_start(step), BLOCK)
        return pltpu.make_async_copy(counts.at[rows], loaded.at[rows], load_sem.at[step])

    w_copy = pltpu.make_async_copy(weight, w_buf, w_sem)
    w_copy.start()
    for step in range(4):
        load(step).start()

    own_slot = (z * 16 + plane) * 2 + core
    lists[own_slot] = jnp.zeros((1, 128), i32)
    for cell in range(4):
        lists[own_slot, :, cell * SLOT : cell * SLOT + K] = neighbours[cell : cell + 1, :]

    def list_core():
        return pltpu.make_async_remote_copy(
            src_ref=lists.at[own_slot], dst_ref=lists.at[own_slot],
            send_sem=list_ss.at[0], recv_sem=list_rs.at[0],
            device_id=sibling, device_id_type=MESH,
        )

    def list_plane(step):
        px, py = plane_at(step)
        part = lists.at[pl.ds((z * 16 + plane) * 2, 2)]
        return pltpu.make_async_remote_copy(
            src_ref=part, dst_ref=part,
            send_sem=list_ss.at[step], recv_sem=list_rs.at[step],
            device_id=device(px, py, z, core), device_id_type=MESH,
        )

    def list_column(step):
        part = lists.at[pl.ds(z * 32, 32)]
        return pltpu.make_async_remote_copy(
            src_ref=part, dst_ref=part,
            send_sem=list_ss.at[15 + step], recv_sem=list_rs.at[15 + step],
            device_id=device(x, y, (z + step) % 8, core), device_id_type=MESH,
        )

    def core_copy(step):
        rows = rows_of(BLOCK * step, BLOCK)
        return pltpu.make_async_remote_copy(
            src_ref=core_send.at[rows], dst_ref=core_recv.at[rows],
            send_sem=core_ss.at[step], recv_sem=core_rs.at[step],
            device_id=sibling, device_id_type=MESH,
        )

    def plane_copy(step):
        px, py = plane_at(step)
        return pltpu.make_async_remote_copy(
            src_ref=plane_send.at[rows_of((px * 4 + py) * PIECE, PIECE)], dst_ref=plane_recv.at[step],
            send_sem=plane_ss.at[step], recv_sem=plane_rs.at[step],
            device_id=device(px, py, z, core), device_id_type=MESH,
        )

    def column_copy(step):
        return pltpu.make_async_remote_copy(
            src_ref=column.at[z], dst_ref=column.at[z],
            send_sem=z_ss.at[step], recv_sem=z_rs.at[step],
            device_id=device(x, y, (z + step) % 8, core), device_id_type=MESH,
        )

    own_rows = rows_of(core * HALF + plane * PIECE, PIECE)

    def out_copy(step):
        px, py = plane_at(step)
        return pltpu.make_async_remote_copy(
            src_ref=hidden.at[own_rows], dst_ref=hidden.at[own_rows],
            send_sem=out_ss.at[step], recv_sem=out_rs.at[step],
            device_id=device(px, py, z, core), device_id_type=MESH,
        )

    def fwd_copy(step):
        px, py = plane_from(step)
        rows = rows_of(core * HALF + (px * 4 + py) * PIECE, PIECE)
        return pltpu.make_async_remote_copy(
            src_ref=hidden.at[rows], dst_ref=hidden.at[rows],
            send_sem=fwd_ss.at[step], recv_sem=fwd_rs.at[step],
            device_id=sibling, device_id_type=MESH,
        )

    def each(first, last, what):
        def run(step, carry):
            what(step)
            return carry

        lax.fori_loop(first, last, run, 0)

    pl.semaphore_wait(barrier, 23)
    list_core().start()
    w_copy.wait()

    def peak_block(step, carry):
        start = block_start(step)
        rows = rows_of(start, BLOCK)
        load(step).wait()
        keep = tile_mask[rows, :].astype(f32).astype(bf16)
        for tile in range(LOCAL // TILE):
            lanes = slice(tile * TILE, (tile + 1) * TILE)
            masked[rows, lanes] = loaded[rows, lanes] * jnp.broadcast_to(
                keep[:, tile : tile + 1], (BLOCK, TILE)
            )
        term = jnp.dot(masked[rows, :], w_buf[...], preferred_element_type=f32)

        @pl.when(step < 2)
        def _():
            core_send[rows_of(BLOCK * step, BLOCK), :] = term.astype(bf16)
            core_copy(step).start()

        @pl.when(step >= 2)
        def _():
            partial[rows_of(BLOCK * (step - 2), BLOCK), :] = term

        return carry

    lax.fori_loop(0, 4, peak_block, 0)

    list_core().wait()
    each(1, 16, lambda step: list_plane(step).start())
    for step in range(2):
        core_copy(step).wait()
    for part in range(4):
        rows = slice(part * 128, (part + 1) * 128)
        plane_send[rows, :] = (partial[rows, :] + core_recv[rows, :].astype(f32)).astype(bf16)
    each(1, 16, lambda step: plane_copy(step).start())
    each(1, 16, lambda step: list_plane(step).wait())
    each(1, 8, lambda step: list_column(step).start())

    def turn(step, carry):
        rows = rows_of(step * 128, 128)
        for tile in range(LOCAL // TILE):
            lanes = slice(tile * TILE, (tile + 1) * TILE)
            turned[lanes, rows] = masked[rows, lanes].T
        return carry

    lax.fori_loop(0, CELLS // 128, turn, 0)
    turned_store = pltpu.make_async_copy(turned, turned_out, store_sem.at[0])
    turned_store.start()

    def add_plane(step, total):
        plane_copy(step).wait()
        return total + plane_recv[step].astype(f32)

    total = lax.fori_loop(1, 16, add_plane, plane_send[rows_of(plane * PIECE, PIECE), :].astype(f32))
    column[z] = total.astype(bf16)
    each(1, 8, lambda step: column_copy(step).start())
    each(1, 8, lambda step: list_column(step).wait())

    by_slot = lists[:, 0, :].astype(f32).T
    place = lax.broadcasted_iota(i32, (CELLS // 4, 1), 0)
    at_core, at_y, at_x, at_z = place % 2, (place // 2) % 4, (place // 8) % 4, place // 32
    holder = (((at_z % 2) * 4 + at_x) * 2 + at_core) * 16 + at_y * 4 + at_z // 2
    cells = lax.broadcasted_iota(i32, (CELLS // 4, CELLS), 1)
    gathered = jnp.zeros((2 * SLOT, CELLS), f32)
    for cell in range(4):
        chosen = (holder * 4 + cell == cells).astype(f32).astype(bf16)
        entry = by_slot[cell * SLOT : (cell + 1) * SLOT, :]
        high = jnp.floor(entry * (1.0 / 32.0))
        low = entry - 32.0 * high
        gathered += jnp.dot(
            jnp.concatenate([high, low], axis=0).astype(bf16), chosen, preferred_element_type=f32
        )
    list_rows[...] = 32.0 * gathered[:SLOT, :] + gathered[SLOT:, :]

    for part in range(CELLS // 128):
        lanes = slice(part * 128, (part + 1) * 128)

        def count(step, carry):
            ids = (lax.broadcasted_iota(i32, (64, 128), 0) + step * 64).astype(f32)
            total = jnp.zeros((64, 128), f32)
            for slot in range(K):
                total += jnp.where(list_rows[slot : slot + 1, lanes] == ids, 1.0, 0.0)
            counted[rows_of(step * 64, 64), lanes] = total.astype(bf16)
            return carry

        lax.fori_loop(0, CELLS // 64, count, 0)

    each(1, 8, lambda step: column_copy(step).wait())
    whole = column[0].astype(f32)
    for step in range(1, 8):
        whole += column[step].astype(f32)
    hidden[own_rows, :] = whole.astype(bf16)
    each(1, 16, lambda step: out_copy(step).start())
    fwd_copy(0).start()

    def both(step, carry):
        rows = rows_of(step * 128, 128)
        for part in range(CELLS // 128):
            lanes = slice(part * 128, (part + 1) * 128)
            tallies[rows, lanes] = counted[rows, lanes] + counted[lanes, rows].T
        return carry

    lax.fori_loop(0, CELLS // 128, both, 0)
    tallies_store = pltpu.make_async_copy(tallies, tallies_out, store_sem.at[1])
    tallies_store.start()

    def pass_on(step):
        out_copy(step).wait()
        fwd_copy(step).start()

    each(1, 16, pass_on)
    each(0, 16, lambda step: fwd_copy(step).wait())
    hidden_store = pltpu.make_async_copy(hidden, hidden_out, store_sem.at[2])
    hidden_store.start()
    hidden_store.wait()
    turned_store.wait()
    tallies_store.wait()


def gather_hidden(counts, tile_mask, neighbours, weight):
    any_space = pl.BlockSpec(memory_space=pl.ANY)
    vmem = pl.BlockSpec(memory_space=pltpu.VMEM)
    dma = pltpu.SemaphoreType.DMA
    return pl.pallas_call(
        gather_kernel,
        name="gather_hidden",
        out_shape=(
            jax.ShapeDtypeStruct((CELLS, D), bf16),
            jax.ShapeDtypeStruct((LOCAL, CELLS), bf16),
            jax.ShapeDtypeStruct((CELLS, CELLS), bf16),
        ),
        in_specs=[any_space, vmem, vmem, any_space],
        out_specs=(any_space, any_space, any_space),
        scratch_shapes=[
            pltpu.VMEM((CELLS, LOCAL), bf16),
            pltpu.VMEM((CELLS, LOCAL), bf16),
            pltpu.VMEM((LOCAL, CELLS), bf16),
            pltpu.VMEM((LOCAL, D), bf16),
            pltpu.VMEM((HALF, D), f32),
            pltpu.VMEM((HALF, D), bf16),
            pltpu.VMEM((HALF, D), bf16),
            pltpu.VMEM((HALF, D), bf16),
            pltpu.VMEM((16, PIECE, D), bf16),
            pltpu.VMEM((8, PIECE, D), bf16),
            pltpu.VMEM((CELLS, D), bf16),
            pltpu.VMEM((CELLS // 4, 1, 128), i32),
            pltpu.VMEM((SLOT, CELLS), f32),
            pltpu.VMEM((CELLS, CELLS), bf16),
            pltpu.VMEM((CELLS, CELLS), bf16),
            dma((4,)), dma, dma((2,)), dma((2,)), dma((16,)), dma((16,)), dma((8,)), dma((8,)),
            dma((16,)), dma((16,)), dma((16,)), dma((16,)), dma((23,)), dma((23,)), dma((3,)),
        ],
        compiler_params=pltpu.CompilerParams(
            collective_id=0, has_side_effects=True, vmem_limit_bytes=48 << 20
        ),
        cost_estimate=pl.CostEstimate(
            flops=2 * CELLS * LOCAL * D, bytes_accessed=16 << 20, transcendentals=0
        ),
    )(counts, tile_mask, neighbours, weight)


def across(left, right):
    return lax.dot_general(left, right, (((1,), (1,)), ((), ())), preferred_element_type=f32)


def collapsed(left, right):
    return lax.dot_general(left, right, (((0,), (0,)), ((), ())), preferred_element_type=f32)


def tower_kernel(
    hidden, turned, tallies, gain, w_in, w_out,
    peak_grad, gain_grad, in_grad, out_grad,
    turned_buf, tallies_buf, rounded, slope, activ, unit, length, scale, codes, expo, inverse,
    dproj, dpre, dhidden, peak_buf, load_sem, store_sem,
):
    tallies_copy = pltpu.make_async_copy(tallies, tallies_buf, load_sem.at[0])
    tallies_copy.start()
    turned_copy = pltpu.make_async_copy(turned, turned_buf, load_sem.at[1])
    turned_copy.start()

    step_rows = 256
    steps = CELLS // step_rows

    def forward(step, carry):
        rows = rows_of(step * step_rows, step_rows)
        h = hidden[rows, :].astype(f32)
        s = lax.rsqrt(jnp.mean(h * h, axis=1, keepdims=True) + eps_norm)
        scale[rows, :] = s
        r = (h * s * gain[...]).astype(bf16)
        rounded[rows, :] = r
        v = jnp.dot(r, w_in[...], preferred_element_type=f32)
        t = jnp.tanh(gelu_coef * (v + cubic_coef * v * v * v))
        a = (0.5 * v * (1.0 + t)).astype(bf16)
        activ[rows, :] = a
        slope[rows, :] = 0.5 * (1.0 + t) + 0.5 * v * (1.0 - t * t) * gelu_coef * (
            1.0 + 3.0 * cubic_coef * v * v
        )
        p = jnp.dot(a, w_out[...], preferred_element_type=f32)
        n = lax.rsqrt(jnp.sum(p * p, axis=1, keepdims=True) + eps_norm)
        length[rows, :] = n
        u = p * n
        unit[rows, :] = u
        codes[rows, :] = u.astype(bf16)
        return carry

    lax.fori_loop(0, steps, forward, 0)

    def score(step, column_total):
        rows = rows_of(step * step_rows, step_rows)
        e = jnp.exp(across(codes[rows, :], codes[...]) * sharpness)
        own = lax.broadcasted_iota(i32, (step_rows, CELLS), 0) + step * step_rows
        other = lax.broadcasted_iota(i32, (step_rows, CELLS), 1)
        e = jnp.where(own == other, 0.0, e)
        expo[rows, :] = e
        inverse[rows, :] = 1.0 / jnp.sum(e, axis=1, keepdims=True)
        return column_total + jnp.sum(e, axis=0, keepdims=True)

    column_inverse = 1.0 / lax.fori_loop(0, steps, score, jnp.zeros((1, CELLS), f32))
    tallies_copy.wait()

    def backward(step, gain_total):
        rows = rows_of(step * step_rows, step_rows)
        both = expo[rows, :] * (inverse[rows, :] + column_inverse)
        both = (both - tallies_buf[rows, :].astype(f32) * (1.0 / K)).astype(bf16)
        dcodes = jnp.dot(both, codes[...], preferred_element_type=f32) * sharpness
        u = unit[rows, :]
        dp = (length[rows, :] * (dcodes - u * jnp.sum(u * dcodes, axis=1, keepdims=True))).astype(bf16)
        dproj[rows, :] = dp
        dv = (across(dp, w_out[...]) * slope[rows, :]).astype(bf16)
        dpre[rows, :] = dv
        dround = across(dv, w_in[...])
        s = scale[rows, :]
        normed = hidden[rows, :].astype(f32) * s
        dnorm = dround * gain[...]
        dhidden[rows, :] = (
            s * (dnorm - normed * jnp.mean(dnorm * normed, axis=1, keepdims=True))
        ).astype(bf16)
        return gain_total + jnp.sum(dround * normed, axis=0, keepdims=True)

    gain_grad[...] = lax.fori_loop(0, steps, backward, jnp.zeros((1, D), f32))
    turned_copy.wait()

    def store(step):
        rows = rows_of(step * step_rows, step_rows)
        return pltpu.make_async_copy(peak_buf.at[rows], peak_grad.at[rows], store_sem.at[step])

    def peak(step, carry):
        rows = rows_of(step * step_rows, step_rows)
        peak_buf[rows, :] = jnp.dot(turned_buf[rows, :], dhidden[...], preferred_element_type=f32)
        store(step).start()
        return carry

    lax.fori_loop(0, LOCAL // step_rows, peak, 0)
    in_grad[...] = collapsed(rounded[...], dpre[...])
    out_grad[...] = collapsed(activ[...], dproj[...])

    def stored(step, carry):
        store(step).wait()
        return carry

    lax.fori_loop(0, LOCAL // step_rows, stored, 0)


def tower(hidden, turned, tallies, gain, w_in, w_out):
    any_space = pl.BlockSpec(memory_space=pl.ANY)
    vmem = pl.BlockSpec(memory_space=pltpu.VMEM)
    dma = pltpu.SemaphoreType.DMA
    return pl.pallas_call(
        tower_kernel,
        name="tower",
        out_shape=(
            jax.ShapeDtypeStruct((LOCAL, D), f32),
            jax.ShapeDtypeStruct((1, D), f32),
            jax.ShapeDtypeStruct((D, HID), f32),
            jax.ShapeDtypeStruct((HID, E), f32),
        ),
        in_specs=[vmem, any_space, any_space, vmem, vmem, vmem],
        out_specs=(any_space, vmem, vmem, vmem),
        scratch_shapes=[
            pltpu.VMEM((LOCAL, CELLS), bf16),
            pltpu.VMEM((CELLS, CELLS), bf16),
            pltpu.VMEM((CELLS, D), bf16),
            pltpu.VMEM((CELLS, HID), f32),
            pltpu.VMEM((CELLS, HID), bf16),
            pltpu.VMEM((CELLS, E), f32),
            pltpu.VMEM((CELLS, 1), f32),
            pltpu.VMEM((CELLS, 1), f32),
            pltpu.VMEM((CELLS, E), bf16),
            pltpu.VMEM((CELLS, CELLS), f32),
            pltpu.VMEM((CELLS, 1), f32),
            pltpu.VMEM((CELLS, E), bf16),
            pltpu.VMEM((CELLS, HID), bf16),
            pltpu.VMEM((CELLS, D), bf16),
            pltpu.VMEM((LOCAL, D), f32),
            dma((2,)), dma((8,)),
        ],
        compiler_params=pltpu.CompilerParams(vmem_limit_bytes=48 << 20),
        cost_estimate=pl.CostEstimate(
            flops=6 << 30, bytes_accessed=16 << 20, transcendentals=2 << 20
        ),
    )(hidden, turned, tallies, gain, w_in, w_out)


def body(counts, tile_mask, neighbours, peak_weight, gain, w_in, w_out):
    hidden, turned, tallies = gather_hidden(counts, tile_mask, neighbours, peak_weight)
    peak_grad, gain_grad, in_grad, out_grad = tower(
        hidden, turned, tallies, gain.reshape(1, D), w_in, w_out
    )
    return (peak_grad, gain_grad.reshape(D), in_grad, out_grad)


def solution(mesh):
    cells = P(("grp", "peak"), None)
    peaks = P(None, ("grp", "peak"))
    return jax.shard_map(
        body,
        mesh=mesh,
        in_specs=(peaks, peaks, cells, cells, P(), P(), P()),
        out_specs=(cells, P(), P(), P()),
        check_vma=False,
    )
```

```python
import jax
import jax.numpy as jnp
from jax import lax
from jax.experimental import pallas as pl
from jax.experimental.pallas import tpu as pltpu
from jax.sharding import PartitionSpec as P

TILE = 128
K = 15
CELLS = 1024
D = 512
HID = 512
E = 256
LOCAL = 2048
HALF = CELLS // 2
BLOCK = 256
PIECE = BLOCK // 16
SLOT = 16

sharpness = 5.0
eps_norm = 1e-06
gelu_coef = 0.7978845608
cubic_coef = 0.044715

bf16 = jnp.bfloat16
f32 = jnp.float32
i32 = jnp.int32
MESH = pl.DeviceIdType.MESH


def coordinates():
    grp = lax.axis_index("grp")
    peak = lax.axis_index("peak")
    return (grp // 2) % 4, peak // 4, (peak % 4) * 2 + grp // 8, grp % 2


def device(x, y, z, core):
    return {"grp": ((z % 2) * 4 + x) * 2 + core, "peak": y * 4 + z // 2}


def rows_of(start, size):
    return pl.ds(pl.multiple_of(start, size), size)


STEPS = [(dx, dy) for dx in range(4) for dy in range(4) if dx or dy]


def gather_kernel(
    counts, tile_mask, neighbours, weight,
    hidden_out, turned_out, tallies_out,
    loaded, masked, turned, w_buf, mask_buf, own_lists, core_send, core_recv, plane_send,
    plane_recv, column, hidden, lists, list_rows, counted, tallies,
    load_sem, w_sem, core_ss, core_rs, plane_ss, plane_rs, z_ss, z_rs,
    out_ss, out_rs, fwd_ss, fwd_rs, list_ss, list_rs, store_sem,
):
    x, y, z, core = coordinates()
    plane = x * 4 + y

    def send(source, target, send_sem, recv_sem, to):
        return pltpu.make_async_remote_copy(
            src_ref=source, dst_ref=target, send_sem=send_sem, recv_sem=recv_sem,
            device_id=to, device_id_type=MESH,
        )

    sibling = device(x, y, z, 1 - core)
    plane_to = [((x + dx) % 4, (y + dy) % 4) for dx, dy in STEPS]
    plane_from = [((x + 4 - dx) % 4, (y + 4 - dy) % 4) for dx, dy in STEPS]
    plane_device = [device(px, py, z, core) for px, py in plane_to]
    column_device = [device(x, y, (z + step) % 8, core) for step in range(1, 8)]

    barrier = pltpu.get_barrier_semaphore()
    for other in [sibling] + plane_device + column_device:
        pl.semaphore_signal(barrier, inc=1, device_id=other, device_id_type=MESH)

    def block_start(step):
        return HALF * ((core + 1 + step) % 2) + BLOCK * (step // 2)

    def load(step):
        rows = rows_of(block_start(step), BLOCK)
        return pltpu.make_async_copy(counts.at[rows], loaded.at[rows], load_sem.at[step])

    w_copy = pltpu.make_async_copy(weight, w_buf, w_sem.at[0])
    mask_copy = pltpu.make_async_copy(tile_mask, mask_buf, w_sem.at[1])
    lists_copy = pltpu.make_async_copy(neighbours, own_lists, w_sem.at[2])
    mask_copy.start()
    load(0).start()
    w_copy.start()
    lists_copy.start()
    for step in range(1, 4):
        load(step).start()

    own_slot = (z * 16 + plane) * 2 + core

    def list_copies():
        return (
            [send(lists.at[own_slot], lists.at[own_slot], list_ss.at[0], list_rs.at[0], sibling)],
            [
                send(
                    lists.at[pl.ds((z * 16 + plane) * 2, 2)],
                    lists.at[pl.ds((z * 16 + plane) * 2, 2)],
                    list_ss.at[1 + i], list_rs.at[1 + i], to,
                )
                for i, to in enumerate(plane_device)
            ],
            [
                send(
                    lists.at[pl.ds(z * 32, 32)], lists.at[pl.ds(z * 32, 32)],
                    list_ss.at[16 + i], list_rs.at[16 + i], to,
                )
                for i, to in enumerate(column_device)
            ],
        )

    list_core, list_plane, list_column = list_copies()

    def core_copy(chunk):
        return send(
            core_send.at[chunk], core_recv.at[chunk], core_ss.at[chunk], core_rs.at[chunk], sibling
        )

    def plane_copies(chunk):
        return [
            send(
                plane_send.at[chunk, px * 4 + py], plane_recv.at[chunk, i],
                plane_ss.at[chunk, i], plane_rs.at[chunk, i], plane_device[i],
            )
            for i, (px, py) in enumerate(plane_to)
        ]

    def column_copies(chunk):
        return [
            send(
                column.at[chunk, z], column.at[chunk, z],
                z_ss.at[chunk, i], z_rs.at[chunk, i], to,
            )
            for i, to in enumerate(column_device)
        ]

    def piece_rows(chunk, of):
        return rows_of(core * HALF + chunk * BLOCK + of * PIECE, PIECE)

    def out_copies(chunk):
        rows = piece_rows(chunk, plane)
        return [
            send(hidden.at[rows], hidden.at[rows], out_ss.at[chunk, i], out_rs.at[chunk, i], to)
            for i, to in enumerate(plane_device)
        ]

    def fwd_copy(chunk, i):
        px, py = plane_from[i - 1] if i else (x, y)
        rows = piece_rows(chunk, px * 4 + py)
        return send(
            hidden.at[rows], hidden.at[rows], fwd_ss.at[chunk, i], fwd_rs.at[chunk, i], sibling
        )

    def peak_term(step):
        rows = rows_of(block_start(step), BLOCK)
        load(step).wait()
        keep = mask_buf[:, rows].astype(f32).T.astype(bf16)
        for tile in range(LOCAL // TILE):
            lanes = slice(tile * TILE, (tile + 1) * TILE)
            masked[rows, lanes] = loaded[rows, lanes] * jnp.broadcast_to(
                keep[:, tile : tile + 1], (BLOCK, TILE)
            )
        return jnp.dot(masked[rows, :], w_buf[...], preferred_element_type=f32)

    mask_copy.wait()
    w_copy.wait()

    def peak_chunk(chunk, carry):
        core_send[chunk] = peak_term(2 * chunk).astype(bf16)

        @pl.when(chunk == 0)
        def _():
            lists_copy.wait()
            lists[own_slot] = jnp.zeros((1, 128), i32)
            for cell in range(4):
                lists[own_slot, :, cell * SLOT : cell * SLOT + K] = own_lists[cell : cell + 1, :]
            pl.semaphore_wait(barrier, 23)
            for copy in list_core:
                copy.start()

        core_copy(chunk).start()
        term = peak_term(2 * chunk + 1)
        core_copy(chunk).wait()
        plane_send[chunk] = (term + core_recv[chunk].astype(f32)).astype(bf16).reshape(
            16, PIECE, D
        )
        for copy in plane_copies(chunk):
            copy.start()

        @pl.when(chunk == 0)
        def _():
            for copy in list_core:
                copy.wait()
            for copy in list_plane:
                copy.start()

        return carry

    lax.fori_loop(0, 2, peak_chunk, 0)
    for copy in list_plane:
        copy.wait()
    for copy in list_column:
        copy.start()

    def turn(step, carry):
        rows = rows_of(step * 128, 128)
        for tile in range(LOCAL // TILE):
            lanes = slice(tile * TILE, (tile + 1) * TILE)
            turned[lanes, rows] = masked[rows, lanes].T
        return carry

    def add_plane(chunk):
        total = plane_send[chunk, plane].astype(f32)
        for i, copy in enumerate(plane_copies(chunk)):
            copy.wait()
            total += plane_recv[chunk, i].astype(f32)
        column[chunk, z] = total.astype(bf16)
        for copy in column_copies(chunk):
            copy.start()

    lax.fori_loop(0, 4, turn, 0)
    add_plane(0)
    lax.fori_loop(4, 8, turn, 0)
    turned_store = pltpu.make_async_copy(turned, turned_out, store_sem.at[0])
    turned_store.start()
    add_plane(1)
    for copy in list_column:
        copy.wait()

    by_slot = lists[:, 0, :].astype(f32).T
    place = lax.broadcasted_iota(i32, (CELLS // 4, 1), 0)
    at_core, at_y, at_x, at_z = place % 2, (place // 2) % 4, (place // 8) % 4, place // 32
    holder = (((at_z % 2) * 4 + at_x) * 2 + at_core) * 16 + at_y * 4 + at_z // 2
    cells = lax.broadcasted_iota(i32, (CELLS // 4, CELLS), 1)
    gathered = jnp.zeros((2 * SLOT, CELLS), f32)
    for cell in range(4):
        chosen = (holder * 4 + cell == cells).astype(f32).astype(bf16)
        entry = by_slot[cell * SLOT : (cell + 1) * SLOT, :]
        high = jnp.floor(entry * (1.0 / 32.0))
        low = entry - 32.0 * high
        gathered += jnp.dot(
            jnp.concatenate([high, low], axis=0).astype(bf16), chosen, preferred_element_type=f32
        )
    list_rows[...] = gathered

    def count(part, carry):
        lanes = rows_of(part * 128, 128)
        ids = lax.broadcasted_iota(i32, (32, 128), 0).astype(f32)
        low_is, high = [], []
        for slot in range(K):
            entry = jnp.broadcast_to(list_rows[SLOT + slot : SLOT + slot + 1, lanes], (32, 128))
            low_is.append(jnp.where(entry == ids, 1.0, 0.0).astype(bf16))
            entry = jnp.broadcast_to(list_rows[slot : slot + 1, lanes], (32, 128))
            high.append(entry.astype(bf16))
        none = jnp.zeros((32, 128), bf16)

        def count_rows(step, carry):
            this = jnp.full((32, 128), step.astype(f32), f32).astype(bf16)
            total = none
            for slot in range(K):
                total += jnp.where(high[slot] == this, low_is[slot], none)
            counted[rows_of(step * 32, 32), lanes] = total
            return carry

        return lax.fori_loop(0, CELLS // 32, count_rows, carry, unroll=4)

    def add_column(chunk):
        for copy in column_copies(chunk):
            copy.wait()
        whole = column[chunk, 0].astype(f32)
        for step in range(1, 8):
            whole += column[chunk, step].astype(f32)
        hidden[piece_rows(chunk, plane), :] = whole.astype(bf16)
        for copy in out_copies(chunk):
            copy.start()
        fwd_copy(chunk, 0).start()

    def pass_on(chunk):
        for i, arrived in enumerate(out_copies(chunk)):
            arrived.wait()
            fwd_copy(chunk, i + 1).start()

    lax.fori_loop(0, 3, count, 0)
    add_column(0)
    lax.fori_loop(3, 8, count, 0)
    add_column(1)

    def both(step, carry):
        rows = rows_of(step * 128, 128)
        for part in range(CELLS // 128):
            lanes = slice(part * 128, (part + 1) * 128)
            tallies[rows, lanes] = counted[rows, lanes] + counted[lanes, rows].T
        return carry

    lax.fori_loop(0, CELLS // 128, both, 0)
    tallies_store = pltpu.make_async_copy(tallies, tallies_out, store_sem.at[1])
    tallies_store.start()
    pass_on(0)
    pass_on(1)
    for chunk in range(2):
        for i in range(16):
            fwd_copy(chunk, i).wait()
    hidden_store = pltpu.make_async_copy(hidden, hidden_out, store_sem.at[2])
    hidden_store.start()
    hidden_store.wait()
    turned_store.wait()
    tallies_store.wait()


MASK_T = True


def gather_hidden(counts, tile_mask, neighbours, weight):
    hbm = pl.BlockSpec(memory_space=pltpu.HBM)
    dma = pltpu.SemaphoreType.DMA
    return pl.pallas_call(
        gather_kernel,
        name="gather_hidden",
        out_shape=(
            jax.ShapeDtypeStruct((CELLS, D), bf16),
            jax.ShapeDtypeStruct((LOCAL, CELLS), bf16),
            jax.ShapeDtypeStruct((CELLS, CELLS), bf16),
        ),
        in_specs=[hbm, hbm, hbm, hbm],
        out_specs=(pl.BlockSpec(memory_space=pl.ANY), hbm, hbm),
        scratch_shapes=[
            pltpu.VMEM((CELLS, LOCAL), bf16),
            pltpu.VMEM((CELLS, LOCAL), bf16),
            pltpu.VMEM((LOCAL, CELLS), bf16),
            pltpu.VMEM((LOCAL, D), bf16),
            pltpu.VMEM((LOCAL // TILE, CELLS), i32),
            pltpu.VMEM((4, K), i32),
            pltpu.VMEM((2, BLOCK, D), bf16),
            pltpu.VMEM((2, BLOCK, D), bf16),
            pltpu.VMEM((2, 16, PIECE, D), bf16),
            pltpu.VMEM((2, 15, PIECE, D), bf16),
            pltpu.VMEM((2, 8, PIECE, D), bf16),
            pltpu.VMEM((CELLS, D), bf16),
            pltpu.VMEM((CELLS // 4, 1, 128), i32),
            pltpu.VMEM((2 * SLOT, CELLS), f32),
            pltpu.VMEM((CELLS, CELLS), bf16),
            pltpu.VMEM((CELLS, CELLS), bf16),
            dma((4,)), dma((3,)), dma((2,)), dma((2,)), dma((2, 15)), dma((2, 15)),
            dma((2, 7)), dma((2, 7)), dma((2, 15)), dma((2, 15)), dma((2, 16)), dma((2, 16)),
            dma((23,)), dma((23,)), dma((3,)),
        ],
        compiler_params=pltpu.CompilerParams(
            collective_id=0, has_side_effects=True, vmem_limit_bytes=48 << 20
        ),
        cost_estimate=pl.CostEstimate(
            flops=2 * CELLS * LOCAL * D, bytes_accessed=16 << 20, transcendentals=0
        ),
    )(*(pltpu.with_memory_space_constraint(v, pltpu.HBM) for v in (counts, tile_mask, neighbours, weight)))


def across(left, right):
    return lax.dot_general(left, right, (((1,), (1,)), ((), ())), preferred_element_type=f32)


def collapsed(left, right):
    return lax.dot_general(left, right, (((0,), (0,)), ((), ())), preferred_element_type=f32)


def tower_kernel(
    hidden, turned, tallies, gain, w_in, w_out,
    peak_grad, gain_grad, in_grad, out_grad,
    turned_buf, tallies_buf, rounded, slope, activ, unit, length, scale, codes, expo, inverse,
    dproj, dpre, dhidden, peak_buf, load_sem, store_sem,
):
    tallies_copy = pltpu.make_async_copy(tallies, tallies_buf, load_sem.at[0])
    tallies_copy.start()
    turned_copy = pltpu.make_async_copy(turned, turned_buf, load_sem.at[1])
    turned_copy.start()

    step_rows = 512
    steps = CELLS // step_rows

    def forward(step, carry):
        rows = rows_of(step * step_rows, step_rows)
        h = hidden[rows, :].astype(f32)
        s = lax.rsqrt(jnp.mean(h * h, axis=1, keepdims=True) + eps_norm)
        scale[rows, :] = s
        r = (h * s * gain[...]).astype(bf16)
        rounded[rows, :] = r
        v = jnp.dot(r, w_in[...], preferred_element_type=f32)
        t = jnp.tanh(gelu_coef * (v + cubic_coef * v * v * v))
        a = (0.5 * v * (1.0 + t)).astype(bf16)
        activ[rows, :] = a
        slope[rows, :] = 0.5 * (1.0 + t) + 0.5 * v * (1.0 - t * t) * gelu_coef * (
            1.0 + 3.0 * cubic_coef * v * v
        )
        p = jnp.dot(a, w_out[...], preferred_element_type=f32)
        n = lax.rsqrt(jnp.sum(p * p, axis=1, keepdims=True) + eps_norm)
        length[rows, :] = n
        u = p * n
        unit[rows, :] = u
        codes[rows, :] = u.astype(bf16)
        return carry

    lax.fori_loop(0, steps, forward, 0)

    def score(step, column_total):
        rows = rows_of(step * step_rows, step_rows)
        e = jnp.exp(across(codes[rows, :], codes[...]) * sharpness)
        own = lax.broadcasted_iota(i32, (step_rows, CELLS), 0) + step * step_rows
        other = lax.broadcasted_iota(i32, (step_rows, CELLS), 1)
        e = jnp.where(own == other, 0.0, e)
        expo[rows, :] = e
        inverse[rows, :] = 1.0 / jnp.sum(e, axis=1, keepdims=True)
        return column_total + jnp.sum(e, axis=0, keepdims=True)

    column_inverse = 1.0 / lax.fori_loop(0, steps, score, jnp.zeros((1, CELLS), f32))
    tallies_copy.wait()

    def backward(step, gain_total):
        rows = rows_of(step * step_rows, step_rows)
        both = expo[rows, :] * (inverse[rows, :] + column_inverse)
        both = (both - tallies_buf[rows, :].astype(f32) * (1.0 / K)).astype(bf16)
        dcodes = jnp.dot(both, codes[...], preferred_element_type=f32) * sharpness
        u = unit[rows, :]
        dp = (length[rows, :] * (dcodes - u * jnp.sum(u * dcodes, axis=1, keepdims=True))).astype(bf16)
        dproj[rows, :] = dp
        dv = (across(dp, w_out[...]) * slope[rows, :]).astype(bf16)
        dpre[rows, :] = dv
        dround = across(dv, w_in[...])
        s = scale[rows, :]
        normed = hidden[rows, :].astype(f32) * s
        dnorm = dround * gain[...]
        dhidden[rows, :] = (
            s * (dnorm - normed * jnp.mean(dnorm * normed, axis=1, keepdims=True))
        ).astype(bf16)
        return gain_total + jnp.sum(dround * normed, axis=0, keepdims=True)

    gain_grad[...] = lax.fori_loop(0, steps, backward, jnp.zeros((1, D), f32))
    turned_copy.wait()

    def store(step):
        rows = rows_of(step * step_rows, step_rows)
        return pltpu.make_async_copy(peak_buf.at[rows], peak_grad.at[rows], store_sem.at[step])

    def peak(step, carry):
        rows = rows_of(step * step_rows, step_rows)
        peak_buf[rows, :] = jnp.dot(turned_buf[rows, :], dhidden[...], preferred_element_type=f32)
        store(step).start()
        return carry

    lax.fori_loop(0, LOCAL // step_rows, peak, 0)
    in_grad[...] = collapsed(rounded[...], dpre[...])
    out_grad[...] = collapsed(activ[...], dproj[...])

    def stored(step, carry):
        store(step).wait()
        return carry

    lax.fori_loop(0, LOCAL // step_rows, stored, 0)


def tower(hidden, turned, tallies, gain, w_in, w_out):
    any_space = pl.BlockSpec(memory_space=pl.ANY)
    vmem = pl.BlockSpec(memory_space=pltpu.VMEM)
    dma = pltpu.SemaphoreType.DMA
    return pl.pallas_call(
        tower_kernel,
        name="tower",
        out_shape=(
            jax.ShapeDtypeStruct((LOCAL, D), f32),
            jax.ShapeDtypeStruct((1, D), f32),
            jax.ShapeDtypeStruct((D, HID), f32),
            jax.ShapeDtypeStruct((HID, E), f32),
        ),
        in_specs=[vmem, any_space, any_space, vmem, vmem, vmem],
        out_specs=(any_space, vmem, vmem, vmem),
        scratch_shapes=[
            pltpu.VMEM((LOCAL, CELLS), bf16),
            pltpu.VMEM((CELLS, CELLS), bf16),
            pltpu.VMEM((CELLS, D), bf16),
            pltpu.VMEM((CELLS, HID), f32),
            pltpu.VMEM((CELLS, HID), bf16),
            pltpu.VMEM((CELLS, E), f32),
            pltpu.VMEM((CELLS, 1), f32),
            pltpu.VMEM((CELLS, 1), f32),
            pltpu.VMEM((CELLS, E), bf16),
            pltpu.VMEM((CELLS, CELLS), f32),
            pltpu.VMEM((CELLS, 1), f32),
            pltpu.VMEM((CELLS, E), bf16),
            pltpu.VMEM((CELLS, HID), bf16),
            pltpu.VMEM((CELLS, D), bf16),
            pltpu.VMEM((LOCAL, D), f32),
            dma((2,)), dma((8,)),
        ],
        compiler_params=pltpu.CompilerParams(vmem_limit_bytes=46 << 20),
        cost_estimate=pl.CostEstimate(
            flops=6 << 30, bytes_accessed=16 << 20, transcendentals=2 << 20
        ),
    )(hidden, turned, tallies, gain, w_in, w_out)


def body(counts, tile_mask, neighbours, peak_weight, gain, w_in, w_out):
    hidden, turned, tallies = gather_hidden(counts, tile_mask.T, neighbours, peak_weight)
    turned = pltpu.with_memory_space_constraint(turned, pltpu.HBM)
    peak_grad, gain_grad, in_grad, out_grad = tower(
        hidden, turned, tallies, gain.reshape(1, D), w_in, w_out
    )
    return (peak_grad, gain_grad.reshape(D), in_grad, out_grad)


def solution(mesh):
    cells = P(("grp", "peak"), None)
    peaks = P(None, ("grp", "peak"))
    return jax.shard_map(
        body,
        mesh=mesh,
        in_specs=(peaks, peaks, cells, cells, P(), P(), P()),
        out_specs=(cells, P(), P(), P()),
        check_vma=False,
    )
```

```python
import jax
import jax.numpy as jnp
from jax import lax
from jax.experimental import pallas as pl
from jax.experimental.pallas import tpu as pltpu
from jax.sharding import PartitionSpec as P

TILE = 128
K = 15
CELLS = 1024
D = 512
HID = 512
E = 256
LOCAL = 2048
HALF = CELLS // 2
BLOCK = 256
PIECE = BLOCK // 16
SLOT = 16

sharpness = 5.0
eps_norm = 1e-06
gelu_coef = 0.7978845608
cubic_coef = 0.044715

bf16 = jnp.bfloat16
f32 = jnp.float32
i32 = jnp.int32
MESH = pl.DeviceIdType.MESH


def coordinates():
    grp = lax.axis_index("grp")
    peak = lax.axis_index("peak")
    return (grp // 2) % 4, peak // 4, (peak % 4) * 2 + grp // 8, grp % 2


def device(x, y, z, core):
    return {"grp": ((z % 2) * 4 + x) * 2 + core, "peak": y * 4 + z // 2}


def rows_of(start, size):
    return pl.ds(pl.multiple_of(start, size), size)


STEPS = [(dx, dy) for dx in range(4) for dy in range(4) if dx or dy]


def gather_kernel(
    counts, tile_mask, neighbours, weight,
    hidden_out, turned_out, tallies_out,
    loaded, masked, turned, w_buf, mask_buf, own_lists, core_send, core_recv, plane_send,
    plane_recv, column, hidden, lists, list_rows, counted, tallies,
    load_sem, w_sem, core_ss, core_rs, plane_ss, plane_rs, z_ss, z_rs,
    out_ss, out_rs, fwd_ss, fwd_rs, list_ss, list_rs, store_sem,
):
    x, y, z, core = coordinates()
    plane = x * 4 + y

    def send(source, target, send_sem, recv_sem, to):
        return pltpu.make_async_remote_copy(
            src_ref=source, dst_ref=target, send_sem=send_sem, recv_sem=recv_sem,
            device_id=to, device_id_type=MESH,
        )

    sibling = device(x, y, z, 1 - core)
    plane_to = [((x + dx) % 4, (y + dy) % 4) for dx, dy in STEPS]
    plane_from = [((x + 4 - dx) % 4, (y + 4 - dy) % 4) for dx, dy in STEPS]
    plane_device = [device(px, py, z, core) for px, py in plane_to]
    column_device = [device(x, y, (z + step) % 8, core) for step in range(1, 8)]

    barrier = pltpu.get_barrier_semaphore()
    for other in [sibling] + plane_device + column_device:
        pl.semaphore_signal(barrier, inc=1, device_id=other, device_id_type=MESH)

    def block_start(step):
        return HALF * ((core + 1 + step) % 2) + BLOCK * (step // 2)

    def load(step):
        rows = rows_of(block_start(step), BLOCK)
        return pltpu.make_async_copy(counts.at[rows], loaded.at[rows], load_sem.at[step])

    w_copy = pltpu.make_async_copy(weight, w_buf, w_sem.at[0])
    mask_copy = pltpu.make_async_copy(tile_mask, mask_buf, w_sem.at[1])
    lists_copy = pltpu.make_async_copy(neighbours, own_lists, w_sem.at[2])
    mask_copy.start()
    load(0).start()
    w_copy.start()
    lists_copy.start()
    for step in range(1, 4):
        load(step).start()

    own_slot = core * 128 + z * 16 + plane

    list_plane = [
        send(lists.at[own_slot], lists.at[own_slot], list_ss.at[i], list_rs.at[i], to)
        for i, to in enumerate(plane_device)
    ]
    list_layer = lists.at[pl.ds(core * 128 + z * 16, 16)]
    list_column = [
        send(list_layer, list_layer, list_ss.at[15 + i], list_rs.at[15 + i], to)
        for i, to in enumerate(column_device)
    ]
    list_half = lists.at[pl.ds(core * 128, 128)]
    list_core = send(list_half, list_half, list_ss.at[22], list_rs.at[22], sibling)

    def core_copy(chunk):
        return send(
            core_send.at[chunk], core_recv.at[chunk], core_ss.at[chunk], core_rs.at[chunk], sibling
        )

    def plane_copies(chunk):
        return [
            send(
                plane_send.at[chunk, px * 4 + py], plane_recv.at[chunk, i],
                plane_ss.at[chunk, i], plane_rs.at[chunk, i], plane_device[i],
            )
            for i, (px, py) in enumerate(plane_to)
        ]

    def column_copies(chunk):
        return [
            send(
                column.at[chunk, z], column.at[chunk, z],
                z_ss.at[chunk, i], z_rs.at[chunk, i], to,
            )
            for i, to in enumerate(column_device)
        ]

    def piece_rows(chunk, of):
        return rows_of(core * HALF + chunk * BLOCK + of * PIECE, PIECE)

    def out_copies(chunk):
        rows = piece_rows(chunk, plane)
        return [
            send(hidden.at[rows], hidden.at[rows], out_ss.at[chunk, i], out_rs.at[chunk, i], to)
            for i, to in enumerate(plane_device)
        ]

    def fwd_copy(chunk, i):
        px, py = plane_from[i - 1] if i else (x, y)
        rows = piece_rows(chunk, px * 4 + py)
        return send(
            hidden.at[rows], hidden.at[rows], fwd_ss.at[chunk, i], fwd_rs.at[chunk, i], sibling
        )

    def peak_term(step):
        rows = rows_of(block_start(step), BLOCK)
        load(step).wait()
        keep = mask_buf[:, rows].astype(f32).T.astype(bf16)
        for tile in range(LOCAL // TILE):
            lanes = slice(tile * TILE, (tile + 1) * TILE)
            masked[rows, lanes] = loaded[rows, lanes] * jnp.broadcast_to(
                keep[:, tile : tile + 1], (BLOCK, TILE)
            )
        return jnp.dot(masked[rows, :], w_buf[...], preferred_element_type=f32)

    mask_copy.wait()
    w_copy.wait()

    def peak_chunk(chunk, carry):
        core_send[chunk] = peak_term(2 * chunk).astype(bf16)

        @pl.when(chunk == 0)
        def _():
            lists_copy.wait()
            lists[own_slot] = jnp.zeros((1, 128), i32)
            for cell in range(4):
                lists[own_slot, :, cell * SLOT : cell * SLOT + K] = own_lists[cell : cell + 1, :]
            pl.semaphore_wait(barrier, 23)

        core_copy(chunk).start()

        @pl.when(chunk == 0)
        def _():
            for copy in list_plane:
                copy.start()

        term = peak_term(2 * chunk + 1)
        core_copy(chunk).wait()
        plane_send[chunk] = (term + core_recv[chunk].astype(f32)).astype(bf16).reshape(
            16, PIECE, D
        )
        for copy in plane_copies(chunk):
            copy.start()
        return carry

    lax.fori_loop(0, 2, peak_chunk, 0)
    for copy in list_plane:
        copy.wait()
    for copy in list_column:
        copy.start()

    def turn(step, carry):
        rows = rows_of(step * 128, 128)
        for tile in range(LOCAL // TILE):
            lanes = slice(tile * TILE, (tile + 1) * TILE)
            turned[lanes, rows] = masked[rows, lanes].T
        return carry

    def add_plane(chunk):
        total = plane_send[chunk, plane].astype(f32)
        for i, copy in enumerate(plane_copies(chunk)):
            copy.wait()
            total += plane_recv[chunk, i].astype(f32)
        column[chunk, z] = total.astype(bf16)
        for copy in column_copies(chunk):
            copy.start()

    lax.fori_loop(0, 3, turn, 0)
    add_plane(0)
    lax.fori_loop(3, 6, turn, 0)
    add_plane(1)
    for copy in list_column:
        copy.wait()
    list_core.start()
    lax.fori_loop(6, 8, turn, 0)
    turned_store = pltpu.make_async_copy(turned, turned_out, store_sem.at[0])
    turned_store.start()
    list_core.wait()

    by_slot = lists[:, 0, :].astype(f32).T
    place = lax.broadcasted_iota(i32, (CELLS // 4, 1), 0)
    at_core, at_z, at_x, at_y = place // 128, (place // 16) % 8, (place // 4) % 4, place % 4
    holder = (((at_z % 2) * 4 + at_x) * 2 + at_core) * 16 + at_y * 4 + at_z // 2
    cells = lax.broadcasted_iota(i32, (CELLS // 4, CELLS), 1)
    gathered = jnp.zeros((2 * SLOT, CELLS), f32)
    for cell in range(4):
        chosen = (holder * 4 + cell == cells).astype(f32).astype(bf16)
        entry = by_slot[cell * SLOT : (cell + 1) * SLOT, :]
        high = jnp.floor(entry * (1.0 / 32.0))
        low = entry - 32.0 * high
        gathered += jnp.dot(
            jnp.concatenate([high, low], axis=0).astype(bf16), chosen, preferred_element_type=f32
        )
    list_rows[...] = gathered

    def count(part, carry):
        lanes = rows_of(part * 128, 128)
        ids = lax.broadcasted_iota(i32, (32, 128), 0).astype(f32)
        low_is, high = [], []
        for slot in range(K):
            entry = jnp.broadcast_to(list_rows[SLOT + slot : SLOT + slot + 1, lanes], (32, 128))
            low_is.append(jnp.where(entry == ids, 1.0, 0.0).astype(bf16))
            entry = jnp.broadcast_to(list_rows[slot : slot + 1, lanes], (32, 128))
            high.append(entry.astype(bf16))
        none = jnp.zeros((32, 128), bf16)

        def count_rows(step, carry):
            this = jnp.full((32, 128), step.astype(f32), f32).astype(bf16)
            total = none
            for slot in range(K):
                total += jnp.where(high[slot] == this, low_is[slot], none)
            counted[rows_of(step * 32, 32), lanes] = total
            return carry

        return lax.fori_loop(0, CELLS // 32, count_rows, carry, unroll=4)

    def add_column(chunk):
        for copy in column_copies(chunk):
            copy.wait()
        whole = column[chunk, 0].astype(f32)
        for step in range(1, 8):
            whole += column[chunk, step].astype(f32)
        hidden[piece_rows(chunk, plane), :] = whole.astype(bf16)
        for copy in out_copies(chunk):
            copy.start()
        fwd_copy(chunk, 0).start()

    def pass_on(chunk):
        for i, arrived in enumerate(out_copies(chunk)):
            arrived.wait()
            fwd_copy(chunk, i + 1).start()

    lax.fori_loop(0, 3, count, 0)
    add_column(0)
    lax.fori_loop(3, 8, count, 0)
    add_column(1)

    def both(step, carry):
        rows = rows_of(step * 128, 128)
        for part in range(CELLS // 128):
            lanes = slice(part * 128, (part + 1) * 128)
            tallies[rows, lanes] = counted[rows, lanes] + counted[lanes, rows].T
        return carry

    lax.fori_loop(0, CELLS // 128, both, 0)
    tallies_store = pltpu.make_async_copy(tallies, tallies_out, store_sem.at[1])
    tallies_store.start()
    pass_on(0)
    pass_on(1)
    hidden_stores = []
    for chunk in range(2):
        for i in range(16):
            fwd_copy(chunk, i).wait()
        for half in range(2):
            rows = pl.ds(half * HALF + chunk * BLOCK, BLOCK)
            hidden_stores.append(
                pltpu.make_async_copy(
                    hidden.at[rows], hidden_out.at[rows], store_sem.at[2 + 2 * chunk + half]
                )
            )
            hidden_stores[-1].start()
    for copy in hidden_stores:
        copy.wait()
    turned_store.wait()
    tallies_store.wait()


MASK_T = True


def gather_hidden(counts, tile_mask, neighbours, weight):
    hbm = pl.BlockSpec(memory_space=pltpu.HBM)
    dma = pltpu.SemaphoreType.DMA
    return pl.pallas_call(
        gather_kernel,
        name="gather_hidden",
        out_shape=(
            jax.ShapeDtypeStruct((CELLS, D), bf16),
            jax.ShapeDtypeStruct((LOCAL, CELLS), bf16),
            jax.ShapeDtypeStruct((CELLS, CELLS), bf16),
        ),
        in_specs=[hbm, hbm, hbm, hbm],
        out_specs=(pl.BlockSpec(memory_space=pl.ANY), hbm, hbm),
        scratch_shapes=[
            pltpu.VMEM((CELLS, LOCAL), bf16),
            pltpu.VMEM((CELLS, LOCAL), bf16),
            pltpu.VMEM((LOCAL, CELLS), bf16),
            pltpu.VMEM((LOCAL, D), bf16),
            pltpu.VMEM((LOCAL // TILE, CELLS), i32),
            pltpu.VMEM((4, K), i32),
            pltpu.VMEM((2, BLOCK, D), bf16),
            pltpu.VMEM((2, BLOCK, D), bf16),
            pltpu.VMEM((2, 16, PIECE, D), bf16),
            pltpu.VMEM((2, 15, PIECE, D), bf16),
            pltpu.VMEM((2, 8, PIECE, D), bf16),
            pltpu.VMEM((CELLS, D), bf16),
            pltpu.VMEM((CELLS // 4, 1, 128), i32),
            pltpu.VMEM((2 * SLOT, CELLS), f32),
            pltpu.VMEM((CELLS, CELLS), bf16),
            pltpu.VMEM((CELLS, CELLS), bf16),
            dma((4,)), dma((3,)), dma((2,)), dma((2,)), dma((2, 15)), dma((2, 15)),
            dma((2, 7)), dma((2, 7)), dma((2, 15)), dma((2, 15)), dma((2, 16)), dma((2, 16)),
            dma((23,)), dma((23,)), dma((6,)),
        ],
        compiler_params=pltpu.CompilerParams(
            collective_id=0, has_side_effects=True, vmem_limit_bytes=48 << 20
        ),
        cost_estimate=pl.CostEstimate(
            flops=2 * CELLS * LOCAL * D, bytes_accessed=16 << 20, transcendentals=0
        ),
    )(*(pltpu.with_memory_space_constraint(v, pltpu.HBM) for v in (counts, tile_mask, neighbours, weight)))


def across(left, right):
    return lax.dot_general(left, right, (((1,), (1,)), ((), ())), preferred_element_type=f32)


def collapsed(left, right):
    return lax.dot_general(left, right, (((0,), (0,)), ((), ())), preferred_element_type=f32)


def tower_kernel(
    hidden, turned, tallies, gain, w_in, w_out,
    peak_grad, gain_grad, in_grad, out_grad,
    turned_buf, tallies_buf, rounded, slope, activ, unit, length, scale, codes, expo, inverse,
    dproj, dpre, dhidden, peak_buf, in_buf, out_buf, load_sem, store_sem,
):
    tallies_copy = pltpu.make_async_copy(tallies, tallies_buf, load_sem.at[0])
    tallies_copy.start()
    turned_copy = pltpu.make_async_copy(turned, turned_buf, load_sem.at[1])
    turned_copy.start()

    step_rows = 512

    def forward(step, carry):
        rows = rows_of(step * step_rows, step_rows)
        h = hidden[rows, :].astype(f32)
        s = lax.rsqrt(jnp.mean(h * h, axis=1, keepdims=True) + eps_norm)
        scale[rows, :] = s
        r = (h * s * gain[...]).astype(bf16)
        rounded[rows, :] = r
        v = jnp.dot(r, w_in[...], preferred_element_type=f32)
        t = jnp.tanh(gelu_coef * (v + cubic_coef * v * v * v))
        a = (0.5 * v * (1.0 + t)).astype(bf16)
        activ[rows, :] = a
        slope[rows, :] = 0.5 * (1.0 + t) + 0.5 * v * (1.0 - t * t) * gelu_coef * (
            1.0 + 3.0 * cubic_coef * v * v
        )
        p = jnp.dot(a, w_out[...], preferred_element_type=f32)
        n = lax.rsqrt(jnp.sum(p * p, axis=1, keepdims=True) + eps_norm)
        length[rows, :] = n
        u = p * n
        unit[rows, :] = u
        codes[rows, :] = u.astype(bf16)
        return carry

    lax.fori_loop(0, CELLS // step_rows, forward, 0)

    e = jnp.exp(across(codes[...], codes[...]) * sharpness)
    own = lax.broadcasted_iota(i32, (CELLS, CELLS), 0)
    other = lax.broadcasted_iota(i32, (CELLS, CELLS), 1)
    e = jnp.where(own == other, 0.0, e)
    expo[...] = e
    inverse[...] = 1.0 / jnp.sum(e, axis=1, keepdims=True)
    column_inverse = 1.0 / jnp.sum(e, axis=0, keepdims=True)
    tallies_copy.wait()

    both = expo[...] * (inverse[...] + column_inverse)
    both = (both - tallies_buf[...].astype(f32) * (1.0 / K)).astype(bf16)
    dcodes = jnp.dot(both, codes[...], preferred_element_type=f32) * sharpness
    u = unit[...]
    dp = (length[...] * (dcodes - u * jnp.sum(u * dcodes, axis=1, keepdims=True))).astype(bf16)
    dproj[...] = dp
    dv = (across(dp, w_out[...]) * slope[...]).astype(bf16)
    dpre[...] = dv
    dround = across(dv, w_in[...])
    normed = hidden[...].astype(f32) * scale[...]
    dnorm = dround * gain[...]
    dhidden[...] = (
        scale[...] * (dnorm - normed * jnp.mean(dnorm * normed, axis=1, keepdims=True))
    ).astype(bf16)
    gain_grad[...] = jnp.sum(dround * normed, axis=0, keepdims=True)

    in_buf[...] = collapsed(rounded[...], dpre[...])
    in_store = pltpu.make_async_copy(in_buf, in_grad, store_sem.at[4])
    in_store.start()
    out_buf[...] = collapsed(activ[...], dproj[...])
    out_store = pltpu.make_async_copy(out_buf, out_grad, store_sem.at[5])
    out_store.start()
    turned_copy.wait()

    def store(step):
        rows = rows_of(step * step_rows, step_rows)
        return pltpu.make_async_copy(peak_buf.at[rows], peak_grad.at[rows], store_sem.at[step])

    def peak(step, carry):
        rows = rows_of(step * step_rows, step_rows)
        peak_buf[rows, :] = jnp.dot(turned_buf[rows, :], dhidden[...], preferred_element_type=f32)
        store(step).start()
        return carry

    lax.fori_loop(0, LOCAL // step_rows, peak, 0)
    in_store.wait()
    out_store.wait()
    def stored(step, carry):
        store(step).wait()
        return carry

    lax.fori_loop(0, LOCAL // step_rows, stored, 0)


def tower(hidden, turned, tallies, gain, w_in, w_out):
    any_space = pl.BlockSpec(memory_space=pl.ANY)
    vmem = pl.BlockSpec(memory_space=pltpu.VMEM)
    dma = pltpu.SemaphoreType.DMA
    return pl.pallas_call(
        tower_kernel,
        name="tower",
        out_shape=(
            jax.ShapeDtypeStruct((LOCAL, D), f32),
            jax.ShapeDtypeStruct((1, D), f32),
            jax.ShapeDtypeStruct((D, HID), f32),
            jax.ShapeDtypeStruct((HID, E), f32),
        ),
        in_specs=[vmem, any_space, any_space, vmem, vmem, vmem],
        out_specs=(any_space, vmem, any_space, any_space),
        scratch_shapes=[
            pltpu.VMEM((LOCAL, CELLS), bf16),
            pltpu.VMEM((CELLS, CELLS), bf16),
            pltpu.VMEM((CELLS, D), bf16),
            pltpu.VMEM((CELLS, HID), f32),
            pltpu.VMEM((CELLS, HID), bf16),
            pltpu.VMEM((CELLS, E), f32),
            pltpu.VMEM((CELLS, 1), f32),
            pltpu.VMEM((CELLS, 1), f32),
            pltpu.VMEM((CELLS, E), bf16),
            pltpu.VMEM((CELLS, CELLS), f32),
            pltpu.VMEM((CELLS, 1), f32),
            pltpu.VMEM((CELLS, E), bf16),
            pltpu.VMEM((CELLS, HID), bf16),
            pltpu.VMEM((CELLS, D), bf16),
            pltpu.VMEM((LOCAL, D), f32),
            pltpu.VMEM((D, HID), f32),
            pltpu.VMEM((HID, E), f32),
            dma((2,)), dma((6,)),
        ],
        compiler_params=pltpu.CompilerParams(vmem_limit_bytes=46 << 20),
        cost_estimate=pl.CostEstimate(
            flops=6 << 30, bytes_accessed=16 << 20, transcendentals=2 << 20
        ),
    )(hidden, turned, tallies, gain, w_in, w_out)


def body(counts, tile_mask, neighbours, peak_weight, gain, w_in, w_out):
    hidden, turned, tallies = gather_hidden(counts, tile_mask.T, neighbours, peak_weight)
    turned = pltpu.with_memory_space_constraint(turned, pltpu.HBM)
    peak_grad, gain_grad, in_grad, out_grad = tower(
        hidden, turned, tallies, gain.reshape(1, D), w_in, w_out
    )
    return (peak_grad, gain_grad.reshape(D), in_grad, out_grad)


def solution(mesh):
    cells = P(("grp", "peak"), None)
    peaks = P(None, ("grp", "peak"))
    return jax.shard_map(
        body,
        mesh=mesh,
        in_specs=(peaks, peaks, cells, cells, P(), P(), P()),
        out_specs=(cells, P(), P(), P()),
        check_vma=False,
    )
```

```python
import jax
import jax.numpy as jnp
from jax import lax
from jax.experimental import pallas as pl
from jax.experimental.pallas import tpu as pltpu
from jax.sharding import PartitionSpec as P

TILE = 128
K = 15
CELLS = 1024
D = 512
HID = 512
E = 256
LOCAL = 2048
HALF = CELLS // 2
BLOCK = 256
PIECE = BLOCK // 16
SLOT = 16

sharpness = 5.0
eps_norm = 1e-06
gelu_coef = 0.7978845608
cubic_coef = 0.044715
log2_e = 1.4426950408889634

bf16 = jnp.bfloat16
f32 = jnp.float32
i32 = jnp.int32
MESH = pl.DeviceIdType.MESH


def coordinates():
    grp = lax.axis_index("grp")
    peak = lax.axis_index("peak")
    return (grp // 2) % 4, peak // 4, (peak % 4) * 2 + grp // 8, grp % 2


def device(x, y, z, core):
    return {"grp": ((z % 2) * 4 + x) * 2 + core, "peak": y * 4 + z // 2}


def rows_of(start, size):
    return pl.ds(pl.multiple_of(start, size), size)


STEPS = [(dx, dy) for dx in range(4) for dy in range(4) if dx or dy]


def gather_kernel(
    counts, tile_mask, neighbours, weight,
    hidden_out, turned_out, tallies_out,
    loaded, masked, turned, w_buf, mask_buf, own_lists, core_send, core_recv, plane_send,
    plane_recv, column, own_piece, lists, list_rows, counted, tallies,
    load_sem, w_sem, core_ss, core_rs, plane_ss, plane_rs, z_ss, z_rs,
    out_ss, out_rs, fwd_ss, fwd_rs, list_ss, list_rs, store_sem,
):
    x, y, z, core = coordinates()
    plane = x * 4 + y

    def send(source, target, send_sem, recv_sem, to):
        return pltpu.make_async_remote_copy(
            src_ref=source, dst_ref=target, send_sem=send_sem, recv_sem=recv_sem,
            device_id=to, device_id_type=MESH,
        )

    sibling = device(x, y, z, 1 - core)
    plane_to = [((x + dx) % 4, (y + dy) % 4) for dx, dy in STEPS]
    plane_device = [device(px, py, z, core) for px, py in plane_to]
    column_device = [device(x, y, (z + step) % 8, core) for step in range(1, 8)]

    barrier = pltpu.get_barrier_semaphore()
    for other in [sibling] + plane_device + column_device:
        pl.semaphore_signal(barrier, inc=1, device_id=other, device_id_type=MESH)

    def block_start(step):
        return HALF * ((core + 1 + step) % 2) + BLOCK * (step // 2)

    def load(step):
        rows = rows_of(block_start(step), BLOCK)
        return pltpu.make_async_copy(counts.at[rows], loaded.at[rows], load_sem.at[step])

    w_copy = pltpu.make_async_copy(weight, w_buf, w_sem.at[0])
    mask_copy = pltpu.make_async_copy(tile_mask, mask_buf, w_sem.at[1])
    lists_copy = pltpu.make_async_copy(neighbours, own_lists, w_sem.at[2])
    mask_copy.start()
    load(0).start()
    w_copy.start()
    lists_copy.start()
    for step in range(1, 4):
        load(step).start()

    own_slot = core * 128 + z * 16 + plane

    list_plane = [
        send(lists.at[own_slot], lists.at[own_slot], list_ss.at[i], list_rs.at[i], to)
        for i, to in enumerate(plane_device)
    ]
    list_layer = lists.at[pl.ds(core * 128 + z * 16, 16)]
    list_column = [
        send(list_layer, list_layer, list_ss.at[15 + i], list_rs.at[15 + i], to)
        for i, to in enumerate(column_device)
    ]
    list_half = lists.at[pl.ds(core * 128, 128)]
    list_core = send(list_half, list_half, list_ss.at[22], list_rs.at[22], sibling)

    def core_copy(chunk):
        return send(
            core_send.at[chunk], core_recv.at[chunk], core_ss.at[chunk], core_rs.at[chunk], sibling
        )

    def plane_copies(chunk):
        return [
            send(
                plane_send.at[chunk, px * 4 + py], plane_recv.at[chunk, i],
                plane_ss.at[chunk, i], plane_rs.at[chunk, i], plane_device[i],
            )
            for i, (px, py) in enumerate(plane_to)
        ]

    def column_copies(chunk):
        return [
            send(
                column.at[chunk, z], column.at[chunk, z],
                z_ss.at[chunk, i], z_rs.at[chunk, i], to,
            )
            for i, to in enumerate(column_device)
        ]

    def piece_rows(chunk, of):
        return rows_of(core * HALF + chunk * BLOCK + of * PIECE, PIECE)

    def keep_piece(chunk):
        return pltpu.make_async_copy(
            own_piece.at[chunk], hidden_out.at[piece_rows(chunk, plane)], store_sem.at[2 + chunk]
        )

    def out_copies(chunk):
        rows = piece_rows(chunk, plane)
        return [
            send(
                own_piece.at[chunk], hidden_out.at[rows],
                out_ss.at[chunk, i], out_rs.at[chunk, i], to,
            )
            for i, to in enumerate(plane_device)
        ]

    def fwd_copy(chunk, dx):
        start = core * HALF + chunk * BLOCK + ((x + 4 - dx) % 4) * 4 * PIECE
        rows = rows_of(start, 4 * PIECE)
        return send(
            hidden_out.at[rows], hidden_out.at[rows],
            fwd_ss.at[chunk, dx], fwd_rs.at[chunk, dx], sibling,
        )

    def peak_term(step):
        rows = rows_of(block_start(step), BLOCK)
        load(step).wait()
        keep = mask_buf[:, rows].astype(f32).T.astype(bf16)
        for tile in range(LOCAL // TILE):
            lanes = slice(tile * TILE, (tile + 1) * TILE)
            masked[rows, lanes] = loaded[rows, lanes] * jnp.broadcast_to(
                keep[:, tile : tile + 1], (BLOCK, TILE)
            )
        return jnp.dot(masked[rows, :], w_buf[...], preferred_element_type=f32)

    mask_copy.wait()
    w_copy.wait()

    def peak_chunk(chunk, carry):
        core_send[chunk] = peak_term(2 * chunk).astype(bf16)

        @pl.when(chunk == 0)
        def _():
            lists_copy.wait()
            lists[own_slot] = jnp.zeros((1, 128), i32)
            for cell in range(4):
                lists[own_slot, :, cell * SLOT : cell * SLOT + K] = own_lists[cell : cell + 1, :]
            pl.semaphore_wait(barrier, 23)

        core_copy(chunk).start()

        @pl.when(chunk == 0)
        def _():
            for copy in list_plane:
                copy.start()

        term = peak_term(2 * chunk + 1)
        core_copy(chunk).wait()
        plane_send[chunk] = (term + core_recv[chunk].astype(f32)).astype(bf16).reshape(
            16, PIECE, D
        )
        for copy in plane_copies(chunk):
            copy.start()
        return carry

    lax.fori_loop(0, 2, peak_chunk, 0)
    for copy in list_plane:
        copy.wait()
    for copy in list_column:
        copy.start()

    def turn(step, carry):
        rows = rows_of(step * 128, 128)
        for tile in range(LOCAL // TILE):
            lanes = slice(tile * TILE, (tile + 1) * TILE)
            turned[lanes, rows] = masked[rows, lanes].T
        return carry

    def add_plane(chunk):
        total = plane_send[chunk, plane].astype(f32)
        for i, copy in enumerate(plane_copies(chunk)):
            copy.wait_recv()
            total += plane_recv[chunk, i].astype(f32)
        column[chunk, z] = total.astype(bf16)
        for copy in column_copies(chunk):
            copy.start()

    lax.fori_loop(0, 3, turn, 0)
    add_plane(0)
    lax.fori_loop(3, 6, turn, 0)
    add_plane(1)
    for copy in list_column:
        copy.wait()
    list_core.start()
    lax.fori_loop(6, 8, turn, 0)
    turned_store = pltpu.make_async_copy(turned, turned_out, store_sem.at[0])
    turned_store.start()
    list_core.wait()

    by_slot = lists[:, 0, :].astype(f32).T
    place = lax.broadcasted_iota(i32, (CELLS // 4, 1), 0)
    at_core, at_z, at_x, at_y = place // 128, (place // 16) % 8, (place // 4) % 4, place % 4
    holder = (((at_z % 2) * 4 + at_x) * 2 + at_core) * 16 + at_y * 4 + at_z // 2
    cells = lax.broadcasted_iota(i32, (CELLS // 4, CELLS), 1)
    gathered = jnp.zeros((2 * SLOT, CELLS), f32)
    for cell in range(4):
        chosen = (holder * 4 + cell == cells).astype(f32).astype(bf16)
        entry = by_slot[cell * SLOT : (cell + 1) * SLOT, :]
        high = jnp.floor(entry * (1.0 / 32.0))
        low = entry - 32.0 * high
        gathered += jnp.dot(
            jnp.concatenate([high, low], axis=0).astype(bf16), chosen, preferred_element_type=f32
        )
    list_rows[...] = gathered

    def count(part, carry):
        lanes = rows_of(part * 128, 128)
        ids = lax.broadcasted_iota(i32, (32, 128), 0).astype(f32)
        low_is, high = [], []
        for slot in range(K):
            entry = jnp.broadcast_to(list_rows[SLOT + slot : SLOT + slot + 1, lanes], (32, 128))
            low_is.append(jnp.where(entry == ids, 1.0, 0.0).astype(bf16))
            entry = jnp.broadcast_to(list_rows[slot : slot + 1, lanes], (32, 128))
            high.append(entry.astype(bf16))
        none = jnp.zeros((32, 128), bf16)

        def count_rows(step, carry):
            this = jnp.full((32, 128), step.astype(f32), f32).astype(bf16)
            total = none
            for slot in range(K):
                total += jnp.where(high[slot] == this, low_is[slot], none)
            counted[rows_of(step * 32, 32), lanes] = total
            return carry

        return lax.fori_loop(0, CELLS // 32, count_rows, carry, unroll=4)

    def add_column(chunk):
        for copy in column_copies(chunk):
            copy.wait_recv()
        whole = column[chunk, 0].astype(f32)
        for step in range(1, 8):
            whole += column[chunk, step].astype(f32)
        own_piece[chunk] = whole.astype(bf16)
        for copy in out_copies(chunk):
            copy.start()
        keep_piece(chunk).start()

    def pass_on(chunk):
        arrived = out_copies(chunk)
        keep_piece(chunk).wait()
        for dx in range(4):
            for i, step in enumerate(STEPS):
                if step[0] == dx:
                    arrived[i].wait_recv()
            fwd_copy(chunk, dx).start()

    lax.fori_loop(0, 3, count, 0)
    add_column(0)
    lax.fori_loop(3, 8, count, 0)
    add_column(1)

    def both(step, carry):
        rows = rows_of(step * 128, 128)
        for part in range(CELLS // 128):
            lanes = slice(part * 128, (part + 1) * 128)
            tallies[rows, lanes] = counted[rows, lanes] + counted[lanes, rows].T
        return carry

    lax.fori_loop(0, CELLS // 128, both, 0)
    tallies_store = pltpu.make_async_copy(tallies, tallies_out, store_sem.at[1])
    tallies_store.start()
    pass_on(0)
    pass_on(1)
    for chunk in range(2):
        for copy in plane_copies(chunk) + column_copies(chunk) + out_copies(chunk):
            copy.wait_send()
    for chunk in range(2):
        for dx in range(4):
            fwd_copy(chunk, dx).wait()
    turned_store.wait()
    tallies_store.wait()


MASK_T = True


def gather_hidden(counts, tile_mask, neighbours, weight):
    hbm = pl.BlockSpec(memory_space=pltpu.HBM)
    dma = pltpu.SemaphoreType.DMA
    return pl.pallas_call(
        gather_kernel,
        name="gather_hidden",
        out_shape=(
            jax.ShapeDtypeStruct((CELLS, D), bf16),
            jax.ShapeDtypeStruct((LOCAL, CELLS), bf16),
            jax.ShapeDtypeStruct((CELLS, CELLS), bf16),
        ),
        in_specs=[hbm, hbm, hbm, hbm],
        out_specs=(pl.BlockSpec(memory_space=pl.ANY), hbm, hbm),
        scratch_shapes=[
            pltpu.VMEM((CELLS, LOCAL), bf16),
            pltpu.VMEM((CELLS, LOCAL), bf16),
            pltpu.VMEM((LOCAL, CELLS), bf16),
            pltpu.VMEM((LOCAL, D), bf16),
            pltpu.VMEM((LOCAL // TILE, CELLS), i32),
            pltpu.VMEM((4, K), i32),
            pltpu.VMEM((2, BLOCK, D), bf16),
            pltpu.VMEM((2, BLOCK, D), bf16),
            pltpu.VMEM((2, 16, PIECE, D), bf16),
            pltpu.VMEM((2, 15, PIECE, D), bf16),
            pltpu.VMEM((2, 8, PIECE, D), bf16),
            pltpu.VMEM((2, PIECE, D), bf16),
            pltpu.VMEM((CELLS // 4, 1, 128), i32),
            pltpu.VMEM((2 * SLOT, CELLS), f32),
            pltpu.VMEM((CELLS, CELLS), bf16),
            pltpu.VMEM((CELLS, CELLS), bf16),
            dma((4,)), dma((3,)), dma((2,)), dma((2,)), dma((2, 15)), dma((2, 15)),
            dma((2, 7)), dma((2, 7)), dma((2, 15)), dma((2, 15)), dma((2, 4)), dma((2, 4)),
            dma((23,)), dma((23,)), dma((4,)),
        ],
        compiler_params=pltpu.CompilerParams(
            collective_id=0, has_side_effects=True, vmem_limit_bytes=48 << 20
        ),
        cost_estimate=pl.CostEstimate(
            flops=2 * CELLS * LOCAL * D, bytes_accessed=16 << 20, transcendentals=0
        ),
    )(*(pltpu.with_memory_space_constraint(v, pltpu.HBM) for v in (counts, tile_mask, neighbours, weight)))


def across(left, right):
    return lax.dot_general(left, right, (((1,), (1,)), ((), ())), preferred_element_type=f32)


def collapsed(left, right):
    return lax.dot_general(left, right, (((0,), (0,)), ((), ())), preferred_element_type=f32)


def tower_kernel(
    hidden, turned, tallies, gain, w_in, w_out,
    peak_grad, gain_grad, in_grad, out_grad,
    turned_buf, tallies_buf, rounded, slope, activ, unit, length, scale, codes, expo, inverse,
    dproj, dpre, dhidden, peak_buf, in_buf, out_buf, load_sem, store_sem,
):
    tallies_copy = pltpu.make_async_copy(tallies, tallies_buf, load_sem.at[0])
    tallies_copy.start()
    turned_copy = pltpu.make_async_copy(turned, turned_buf, load_sem.at[1])
    turned_copy.start()

    step_rows = 512

    def forward(step, carry):
        rows = rows_of(step * step_rows, step_rows)
        h = hidden[rows, :].astype(f32)
        s = lax.rsqrt(jnp.mean(h * h, axis=1, keepdims=True) + eps_norm)
        scale[rows, :] = s
        r = (h * s * gain[...]).astype(bf16)
        rounded[rows, :] = r
        v = jnp.dot(r, w_in[...], preferred_element_type=f32)
        square = v * v
        t = jnp.tanh(v * (gelu_coef + (gelu_coef * cubic_coef) * square))
        half_v = 0.5 * v
        a = (half_v + half_v * t).astype(bf16)
        activ[rows, :] = a
        slope[rows, :] = (0.5 + 0.5 * t) + half_v * (1.0 - t * t) * (
            gelu_coef + (3.0 * gelu_coef * cubic_coef) * square
        )
        p = jnp.dot(a, w_out[...], preferred_element_type=f32)
        n = lax.rsqrt(jnp.sum(p * p, axis=1, keepdims=True) + eps_norm)
        length[rows, :] = n
        u = p * n
        unit[rows, :] = u
        codes[rows, :] = u.astype(bf16)
        return carry

    lax.fori_loop(0, CELLS // step_rows, forward, 0)

    expo[...] = jnp.exp2(across(codes[...], codes[...]) * (sharpness * log2_e))
    diagonal = lax.broadcasted_iota(i32, (128, 128), 0) == lax.broadcasted_iota(i32, (128, 128), 1)
    for part in range(CELLS // 128):
        block = slice(part * 128, (part + 1) * 128)
        expo[block, block] = jnp.where(diagonal, 0.0, expo[block, block])
    e = expo[...]
    inverse[...] = 1.0 / jnp.sum(e, axis=1, keepdims=True)
    column_inverse = 1.0 / jnp.sum(e, axis=0, keepdims=True)
    tallies_copy.wait()

    both = expo[...] * (inverse[...] + column_inverse)
    both = (both - tallies_buf[...].astype(f32) * (1.0 / K)).astype(bf16)
    dcodes = jnp.dot(both, codes[...], preferred_element_type=f32) * sharpness
    u = unit[...]
    dp = (length[...] * (dcodes - u * jnp.sum(u * dcodes, axis=1, keepdims=True))).astype(bf16)
    dproj[...] = dp
    dv = (across(dp, w_out[...]) * slope[...]).astype(bf16)
    dpre[...] = dv
    dround = across(dv, w_in[...])
    normed = hidden[...].astype(f32) * scale[...]
    dnorm = dround * gain[...]
    dhidden[...] = (
        scale[...] * (dnorm - normed * jnp.mean(dnorm * normed, axis=1, keepdims=True))
    ).astype(bf16)
    gain_grad[...] = jnp.sum(dround * normed, axis=0, keepdims=True)

    in_buf[...] = collapsed(rounded[...], dpre[...])
    in_store = pltpu.make_async_copy(in_buf, in_grad, store_sem.at[4])
    in_store.start()
    out_buf[...] = collapsed(activ[...], dproj[...])
    out_store = pltpu.make_async_copy(out_buf, out_grad, store_sem.at[5])
    out_store.start()
    turned_copy.wait()

    def store(step):
        rows = rows_of(step * step_rows, step_rows)
        return pltpu.make_async_copy(peak_buf.at[rows], peak_grad.at[rows], store_sem.at[step])

    def peak(step, carry):
        rows = rows_of(step * step_rows, step_rows)
        peak_buf[rows, :] = jnp.dot(turned_buf[rows, :], dhidden[...], preferred_element_type=f32)
        store(step).start()
        return carry

    lax.fori_loop(0, LOCAL // step_rows, peak, 0)
    in_store.wait()
    out_store.wait()
    def stored(step, carry):
        store(step).wait()
        return carry

    lax.fori_loop(0, LOCAL // step_rows, stored, 0)


def tower(hidden, turned, tallies, gain, w_in, w_out):
    any_space = pl.BlockSpec(memory_space=pl.ANY)
    vmem = pl.BlockSpec(memory_space=pltpu.VMEM)
    dma = pltpu.SemaphoreType.DMA
    return pl.pallas_call(
        tower_kernel,
        name="tower",
        out_shape=(
            jax.ShapeDtypeStruct((LOCAL, D), f32),
            jax.ShapeDtypeStruct((1, D), f32),
            jax.ShapeDtypeStruct((D, HID), f32),
            jax.ShapeDtypeStruct((HID, E), f32),
        ),
        in_specs=[vmem, any_space, any_space, vmem, vmem, vmem],
        out_specs=(any_space, vmem, any_space, any_space),
        scratch_shapes=[
            pltpu.VMEM((LOCAL, CELLS), bf16),
            pltpu.VMEM((CELLS, CELLS), bf16),
            pltpu.VMEM((CELLS, D), bf16),
            pltpu.VMEM((CELLS, HID), f32),
            pltpu.VMEM((CELLS, HID), bf16),
            pltpu.VMEM((CELLS, E), f32),
            pltpu.VMEM((CELLS, 1), f32),
            pltpu.VMEM((CELLS, 1), f32),
            pltpu.VMEM((CELLS, E), bf16),
            pltpu.VMEM((CELLS, CELLS), f32),
            pltpu.VMEM((CELLS, 1), f32),
            pltpu.VMEM((CELLS, E), bf16),
            pltpu.VMEM((CELLS, HID), bf16),
            pltpu.VMEM((CELLS, D), bf16),
            pltpu.VMEM((LOCAL, D), f32),
            pltpu.VMEM((D, HID), f32),
            pltpu.VMEM((HID, E), f32),
            dma((2,)), dma((6,)),
        ],
        compiler_params=pltpu.CompilerParams(vmem_limit_bytes=46 << 20),
        cost_estimate=pl.CostEstimate(
            flops=6 << 30, bytes_accessed=16 << 20, transcendentals=2 << 20
        ),
    )(hidden, turned, tallies, gain, w_in, w_out)


def body(counts, tile_mask, neighbours, peak_weight, gain, w_in, w_out):
    hidden, turned, tallies = gather_hidden(counts, tile_mask.T, neighbours, peak_weight)
    turned = pltpu.with_memory_space_constraint(turned, pltpu.HBM)
    peak_grad, gain_grad, in_grad, out_grad = tower(
        hidden, turned, tallies, gain.reshape(1, D), w_in, w_out
    )
    return (peak_grad, gain_grad.reshape(D), in_grad, out_grad)


def solution(mesh):
    cells = P(("grp", "peak"), None)
    peaks = P(None, ("grp", "peak"))
    return jax.shard_map(
        body,
        mesh=mesh,
        in_specs=(peaks, peaks, cells, cells, P(), P(), P()),
        out_specs=(cells, P(), P(), P()),
        check_vma=False,
    )
```

```python
import jax
import jax.numpy as jnp
from jax import lax
from jax.experimental import pallas as pl
from jax.experimental.pallas import tpu as pltpu
from jax.sharding import PartitionSpec as P

TILE = 128
K = 15
CELLS = 1024
D = 512
HID = 512
E = 256
LOCAL = 2048
HALF = CELLS // 2
BLOCK = 256
PIECE = BLOCK // 16
SLOT = 16

sharpness = 5.0
eps_norm = 1e-06
gelu_coef = 0.7978845608
cubic_coef = 0.044715
log2_e = 1.4426950408889634

bf16 = jnp.bfloat16
f32 = jnp.float32
i32 = jnp.int32
MESH = pl.DeviceIdType.MESH


def coordinates():
    grp = lax.axis_index("grp")
    peak = lax.axis_index("peak")
    return (grp // 2) % 4, peak // 4, (peak % 4) * 2 + grp // 8, grp % 2


def device(x, y, z, core):
    return {"grp": ((z % 2) * 4 + x) * 2 + core, "peak": y * 4 + z // 2}


def rows_of(start, size):
    return pl.ds(pl.multiple_of(start, size), size)


STEPS = sorted(
    ((dx, dy) for dx in range(4) for dy in range(4) if dx or dy),
    key=lambda step: -min(step[0], 4 - step[0]) - min(step[1], 4 - step[1]),
)


def gather_kernel(
    counts, tile_mask, neighbours, weight,
    hidden_out, turned_out, tallies_out,
    loaded, masked, turned, w_buf, mask_buf, own_lists, core_send, core_recv, plane_send,
    plane_recv, column, own_piece, lists, list_rows, counted, tallies,
    load_sem, w_sem, core_ss, core_rs, plane_ss, plane_rs, z_ss, z_rs,
    out_ss, out_rs, fwd_ss, fwd_rs, list_ss, list_rs, store_sem,
):
    x, y, z, core = coordinates()
    plane = x * 4 + y

    def send(source, target, send_sem, recv_sem, to):
        return pltpu.make_async_remote_copy(
            src_ref=source, dst_ref=target, send_sem=send_sem, recv_sem=recv_sem,
            device_id=to, device_id_type=MESH,
        )

    sibling = device(x, y, z, 1 - core)
    plane_to = [((x + dx) % 4, (y + dy) % 4) for dx, dy in STEPS]
    plane_device = [device(px, py, z, core) for px, py in plane_to]
    column_device = [device(x, y, (z + step) % 8, core) for step in range(1, 8)]

    barrier = pltpu.get_barrier_semaphore()
    for other in [sibling] + plane_device + column_device:
        pl.semaphore_signal(barrier, inc=1, device_id=other, device_id_type=MESH)

    def block_start(step):
        return HALF * ((core + 1 + step) % 2) + BLOCK * (step // 2)

    def load(step):
        rows = rows_of(block_start(step), BLOCK)
        return pltpu.make_async_copy(counts.at[rows], loaded.at[rows], load_sem.at[step])

    w_copy = pltpu.make_async_copy(weight, w_buf, w_sem.at[0])
    mask_copy = pltpu.make_async_copy(tile_mask, mask_buf, w_sem.at[1])
    lists_copy = pltpu.make_async_copy(neighbours, own_lists, w_sem.at[2])
    mask_copy.start()
    load(0).start()
    w_copy.start()
    lists_copy.start()
    for step in range(1, 4):
        load(step).start()

    own_slot = core * 128 + z * 16 + plane

    list_plane = [
        send(lists.at[own_slot], lists.at[own_slot], list_ss.at[i], list_rs.at[i], to)
        for i, to in enumerate(plane_device)
    ]
    list_layer = lists.at[pl.ds(core * 128 + z * 16, 16)]
    list_column = [
        send(list_layer, list_layer, list_ss.at[15 + i], list_rs.at[15 + i], to)
        for i, to in enumerate(column_device)
    ]
    list_half = lists.at[pl.ds(core * 128, 128)]
    list_core = send(list_half, list_half, list_ss.at[22], list_rs.at[22], sibling)

    def core_copy(chunk):
        return send(
            core_send.at[chunk], core_recv.at[chunk], core_ss.at[chunk], core_rs.at[chunk], sibling
        )

    def plane_copies(chunk):
        return [
            send(
                plane_send.at[chunk, px * 4 + py], plane_recv.at[chunk, i],
                plane_ss.at[chunk, i], plane_rs.at[chunk, i], plane_device[i],
            )
            for i, (px, py) in enumerate(plane_to)
        ]

    def column_copies(chunk):
        return [
            send(
                column.at[chunk, z], column.at[chunk, z],
                z_ss.at[chunk, i], z_rs.at[chunk, i], to,
            )
            for i, to in enumerate(column_device)
        ]

    def piece_rows(chunk, of):
        return rows_of(core * HALF + chunk * BLOCK + of * PIECE, PIECE)

    def keep_piece(chunk):
        return pltpu.make_async_copy(
            own_piece.at[chunk], hidden_out.at[piece_rows(chunk, plane)], store_sem.at[2 + chunk]
        )

    def out_copies(chunk):
        rows = piece_rows(chunk, plane)
        return [
            send(
                own_piece.at[chunk], hidden_out.at[rows],
                out_ss.at[chunk, i], out_rs.at[chunk, i], to,
            )
            for i, to in enumerate(plane_device)
        ]

    def fwd_copy(chunk, dx):
        start = core * HALF + chunk * BLOCK + ((x + 4 - dx) % 4) * 4 * PIECE
        rows = rows_of(start, 4 * PIECE)
        return send(
            hidden_out.at[rows], hidden_out.at[rows],
            fwd_ss.at[chunk, dx], fwd_rs.at[chunk, dx], sibling,
        )

    def peak_term(step):
        rows = rows_of(block_start(step), BLOCK)
        load(step).wait()
        keep = mask_buf[:, rows].astype(f32).T.astype(bf16)
        for tile in range(LOCAL // TILE):
            lanes = slice(tile * TILE, (tile + 1) * TILE)
            masked[rows, lanes] = loaded[rows, lanes] * jnp.broadcast_to(
                keep[:, tile : tile + 1], (BLOCK, TILE)
            )
        return jnp.dot(masked[rows, :], w_buf[...], preferred_element_type=f32)

    mask_copy.wait()
    w_copy.wait()

    def peak_chunk(chunk, carry):
        core_send[chunk] = peak_term(2 * chunk).astype(bf16)

        @pl.when(chunk == 0)
        def _():
            lists_copy.wait()
            lists[own_slot] = jnp.zeros((1, 128), i32)
            for cell in range(4):
                lists[own_slot, :, cell * SLOT : cell * SLOT + K] = own_lists[cell : cell + 1, :]
            pl.semaphore_wait(barrier, 23)

        core_copy(chunk).start()

        @pl.when(chunk == 0)
        def _():
            for copy in list_plane:
                copy.start()

        term = peak_term(2 * chunk + 1)
        core_copy(chunk).wait()
        plane_send[chunk] = (term + core_recv[chunk].astype(f32)).astype(bf16).reshape(
            16, PIECE, D
        )
        for copy in plane_copies(chunk):
            copy.start()
        return carry

    lax.fori_loop(0, 2, peak_chunk, 0)
    for copy in list_plane:
        copy.wait()
    for copy in list_column:
        copy.start()

    def turn(step, carry):
        rows = rows_of(step * 128, 128)
        for tile in range(LOCAL // TILE):
            lanes = slice(tile * TILE, (tile + 1) * TILE)
            turned[lanes, rows] = masked[rows, lanes].T
        return carry

    def add_plane(chunk):
        total = plane_send[chunk, plane].astype(f32)
        for i, copy in enumerate(plane_copies(chunk)):
            copy.wait_recv()
            total += plane_recv[chunk, i].astype(f32)
        column[chunk, z] = total.astype(bf16)
        for copy in column_copies(chunk):
            copy.start()

    lax.fori_loop(0, 3, turn, 0)
    add_plane(0)
    lax.fori_loop(3, 6, turn, 0)
    add_plane(1)
    for copy in list_column:
        copy.wait()
    list_core.start()
    lax.fori_loop(6, 8, turn, 0)
    turned_store = pltpu.make_async_copy(turned, turned_out, store_sem.at[0])
    turned_store.start()
    list_core.wait()

    by_slot = lists[:, 0, :].astype(f32).T
    place = lax.broadcasted_iota(i32, (CELLS // 4, 1), 0)
    at_core, at_z, at_x, at_y = place // 128, (place // 16) % 8, (place // 4) % 4, place % 4
    holder = (((at_z % 2) * 4 + at_x) * 2 + at_core) * 16 + at_y * 4 + at_z // 2
    cells = lax.broadcasted_iota(i32, (CELLS // 4, CELLS), 1)
    gathered = jnp.zeros((2 * SLOT, CELLS), f32)
    for cell in range(4):
        chosen = (holder * 4 + cell == cells).astype(f32).astype(bf16)
        entry = by_slot[cell * SLOT : (cell + 1) * SLOT, :]
        high = jnp.floor(entry * (1.0 / 32.0))
        low = entry - 32.0 * high
        gathered += jnp.dot(
            jnp.concatenate([high, low], axis=0).astype(bf16), chosen, preferred_element_type=f32
        )
    list_rows[...] = gathered

    def count(part, carry):
        lanes = rows_of(part * 128, 128)
        ids = lax.broadcasted_iota(i32, (32, 128), 0).astype(f32)
        low_is, high = [], []
        for slot in range(K):
            entry = jnp.broadcast_to(list_rows[SLOT + slot : SLOT + slot + 1, lanes], (32, 128))
            low_is.append(jnp.where(entry == ids, 1.0, 0.0).astype(bf16))
            entry = jnp.broadcast_to(list_rows[slot : slot + 1, lanes], (32, 128))
            high.append(entry.astype(bf16))
        none = jnp.zeros((32, 128), bf16)

        def count_rows(step, carry):
            this = jnp.full((32, 128), step.astype(f32), f32).astype(bf16)
            total = none
            for slot in range(K):
                total += jnp.where(high[slot] == this, low_is[slot], none)
            counted[rows_of(step * 32, 32), lanes] = total
            return carry

        return lax.fori_loop(0, CELLS // 32, count_rows, carry, unroll=4)

    def add_column(chunk):
        for copy in column_copies(chunk):
            copy.wait_recv()
        whole = column[chunk, 0].astype(f32)
        for step in range(1, 8):
            whole += column[chunk, step].astype(f32)
        own_piece[chunk] = whole.astype(bf16)
        for copy in out_copies(chunk):
            copy.start()
        keep_piece(chunk).start()

    def pass_on(chunk):
        arrived = out_copies(chunk)
        keep_piece(chunk).wait()
        for dx in range(4):
            for i, step in enumerate(STEPS):
                if step[0] == dx:
                    arrived[i].wait_recv()
            fwd_copy(chunk, dx).start()

    lax.fori_loop(0, 3, count, 0)
    add_column(0)
    lax.fori_loop(3, 8, count, 0)
    add_column(1)

    def both(step, carry):
        rows = rows_of(step * 128, 128)
        for part in range(CELLS // 128):
            lanes = slice(part * 128, (part + 1) * 128)
            tallies[rows, lanes] = counted[rows, lanes] + counted[lanes, rows].T
        return carry

    lax.fori_loop(0, CELLS // 128, both, 0)
    tallies_store = pltpu.make_async_copy(tallies, tallies_out, store_sem.at[1])
    tallies_store.start()
    pass_on(0)
    pass_on(1)
    for chunk in range(2):
        for copy in plane_copies(chunk) + column_copies(chunk) + out_copies(chunk):
            copy.wait_send()
    for chunk in range(2):
        for dx in range(4):
            fwd_copy(chunk, dx).wait()
    turned_store.wait()
    tallies_store.wait()


MASK_T = True


def gather_hidden(counts, tile_mask, neighbours, weight):
    hbm = pl.BlockSpec(memory_space=pltpu.HBM)
    dma = pltpu.SemaphoreType.DMA
    return pl.pallas_call(
        gather_kernel,
        name="gather_hidden",
        out_shape=(
            jax.ShapeDtypeStruct((CELLS, D), bf16),
            jax.ShapeDtypeStruct((LOCAL, CELLS), bf16),
            jax.ShapeDtypeStruct((CELLS, CELLS), bf16),
        ),
        in_specs=[hbm, hbm, hbm, hbm],
        out_specs=(pl.BlockSpec(memory_space=pl.ANY), hbm, hbm),
        scratch_shapes=[
            pltpu.VMEM((CELLS, LOCAL), bf16),
            pltpu.VMEM((CELLS, LOCAL), bf16),
            pltpu.VMEM((LOCAL, CELLS), bf16),
            pltpu.VMEM((LOCAL, D), bf16),
            pltpu.VMEM((LOCAL // TILE, CELLS), i32),
            pltpu.VMEM((4, K), i32),
            pltpu.VMEM((2, BLOCK, D), bf16),
            pltpu.VMEM((2, BLOCK, D), bf16),
            pltpu.VMEM((2, 16, PIECE, D), bf16),
            pltpu.VMEM((2, 15, PIECE, D), bf16),
            pltpu.VMEM((2, 8, PIECE, D), bf16),
            pltpu.VMEM((2, PIECE, D), bf16),
            pltpu.VMEM((CELLS // 4, 1, 128), i32),
            pltpu.VMEM((2 * SLOT, CELLS), f32),
            pltpu.VMEM((CELLS, CELLS), bf16),
            pltpu.VMEM((CELLS, CELLS), bf16),
            dma((4,)), dma((3,)), dma((2,)), dma((2,)), dma((2, 15)), dma((2, 15)),
            dma((2, 7)), dma((2, 7)), dma((2, 15)), dma((2, 15)), dma((2, 4)), dma((2, 4)),
            dma((23,)), dma((23,)), dma((4,)),
        ],
        compiler_params=pltpu.CompilerParams(
            collective_id=0, has_side_effects=True, vmem_limit_bytes=48 << 20
        ),
        cost_estimate=pl.CostEstimate(
            flops=2 * CELLS * LOCAL * D, bytes_accessed=16 << 20, transcendentals=0
        ),
    )(*(pltpu.with_memory_space_constraint(v, pltpu.HBM) for v in (counts, tile_mask, neighbours, weight)))


def across(left, right):
    return lax.dot_general(left, right, (((1,), (1,)), ((), ())), preferred_element_type=f32)


def collapsed(left, right):
    return lax.dot_general(left, right, (((0,), (0,)), ((), ())), preferred_element_type=f32)


def tower_kernel(
    hidden, turned, tallies, gain, w_in, w_out,
    peak_grad, gain_grad, in_grad, out_grad,
    turned_buf, tallies_buf, rounded, slope, activ, unit, length, scale, codes, expo, inverse,
    dproj, dpre, dhidden, peak_buf, in_buf, out_buf, load_sem, store_sem,
):
    tallies_copy = pltpu.make_async_copy(tallies, tallies_buf, load_sem.at[0])
    tallies_copy.start()
    turned_copy = pltpu.make_async_copy(turned, turned_buf, load_sem.at[1])
    turned_copy.start()

    step_rows = 512

    def forward(step, carry):
        rows = rows_of(step * step_rows, step_rows)
        h = hidden[rows, :].astype(f32)
        s = lax.rsqrt(jnp.mean(h * h, axis=1, keepdims=True) + eps_norm)
        scale[rows, :] = s
        r = (h * s * gain[...]).astype(bf16)
        rounded[rows, :] = r
        v = jnp.dot(r, w_in[...], preferred_element_type=f32)
        square = v * v
        t = jnp.tanh(v * (gelu_coef + (gelu_coef * cubic_coef) * square))
        half_v = 0.5 * v
        a = (half_v + half_v * t).astype(bf16)
        activ[rows, :] = a
        slope[rows, :] = (0.5 + 0.5 * t) + half_v * (1.0 - t * t) * (
            gelu_coef + (3.0 * gelu_coef * cubic_coef) * square
        )
        p = jnp.dot(a, w_out[...], preferred_element_type=f32)
        n = lax.rsqrt(jnp.sum(p * p, axis=1, keepdims=True) + eps_norm)
        length[rows, :] = n
        u = p * n
        unit[rows, :] = u
        codes[rows, :] = u.astype(bf16)
        return carry

    lax.fori_loop(0, CELLS // step_rows, forward, 0)

    expo[...] = jnp.exp2(across(codes[...], codes[...]) * (sharpness * log2_e))
    diagonal = lax.broadcasted_iota(i32, (128, 128), 0) == lax.broadcasted_iota(i32, (128, 128), 1)
    for part in range(CELLS // 128):
        block = slice(part * 128, (part + 1) * 128)
        expo[block, block] = jnp.where(diagonal, 0.0, expo[block, block])
    e = expo[...]
    inverse[...] = 1.0 / jnp.sum(e, axis=1, keepdims=True)
    column_inverse = 1.0 / jnp.sum(e, axis=0, keepdims=True)
    tallies_copy.wait()

    both = expo[...] * (inverse[...] + column_inverse)
    both = (both - tallies_buf[...].astype(f32) * (1.0 / K)).astype(bf16)
    dcodes = jnp.dot(both, codes[...], preferred_element_type=f32) * sharpness
    u = unit[...]
    dp = (length[...] * (dcodes - u * jnp.sum(u * dcodes, axis=1, keepdims=True))).astype(bf16)
    dproj[...] = dp
    dv = (across(dp, w_out[...]) * slope[...]).astype(bf16)
    dpre[...] = dv
    dround = across(dv, w_in[...])
    normed = hidden[...].astype(f32) * scale[...]
    dnorm = dround * gain[...]
    dhidden[...] = (
        scale[...] * (dnorm - normed * jnp.mean(dnorm * normed, axis=1, keepdims=True))
    ).astype(bf16)
    gain_grad[...] = jnp.sum(dround * normed, axis=0, keepdims=True)

    in_buf[...] = collapsed(rounded[...], dpre[...])
    in_store = pltpu.make_async_copy(in_buf, in_grad, store_sem.at[4])
    in_store.start()
    out_buf[...] = collapsed(activ[...], dproj[...])
    out_store = pltpu.make_async_copy(out_buf, out_grad, store_sem.at[5])
    out_store.start()
    turned_copy.wait()

    def store(step):
        rows = rows_of(step * step_rows, step_rows)
        return pltpu.make_async_copy(peak_buf.at[rows], peak_grad.at[rows], store_sem.at[step])

    def peak(step, carry):
        rows = rows_of(step * step_rows, step_rows)
        peak_buf[rows, :] = jnp.dot(turned_buf[rows, :], dhidden[...], preferred_element_type=f32)
        store(step).start()
        return carry

    lax.fori_loop(0, LOCAL // step_rows, peak, 0)
    in_store.wait()
    out_store.wait()
    def stored(step, carry):
        store(step).wait()
        return carry

    lax.fori_loop(0, LOCAL // step_rows, stored, 0)


def tower(hidden, turned, tallies, gain, w_in, w_out):
    any_space = pl.BlockSpec(memory_space=pl.ANY)
    vmem = pl.BlockSpec(memory_space=pltpu.VMEM)
    dma = pltpu.SemaphoreType.DMA
    return pl.pallas_call(
        tower_kernel,
        name="tower",
        out_shape=(
            jax.ShapeDtypeStruct((LOCAL, D), f32),
            jax.ShapeDtypeStruct((1, D), f32),
            jax.ShapeDtypeStruct((D, HID), f32),
            jax.ShapeDtypeStruct((HID, E), f32),
        ),
        in_specs=[vmem, any_space, any_space, vmem, vmem, vmem],
        out_specs=(any_space, vmem, any_space, any_space),
        scratch_shapes=[
            pltpu.VMEM((LOCAL, CELLS), bf16),
            pltpu.VMEM((CELLS, CELLS), bf16),
            pltpu.VMEM((CELLS, D), bf16),
            pltpu.VMEM((CELLS, HID), f32),
            pltpu.VMEM((CELLS, HID), bf16),
            pltpu.VMEM((CELLS, E), f32),
            pltpu.VMEM((CELLS, 1), f32),
            pltpu.VMEM((CELLS, 1), f32),
            pltpu.VMEM((CELLS, E), bf16),
            pltpu.VMEM((CELLS, CELLS), f32),
            pltpu.VMEM((CELLS, 1), f32),
            pltpu.VMEM((CELLS, E), bf16),
            pltpu.VMEM((CELLS, HID), bf16),
            pltpu.VMEM((CELLS, D), bf16),
            pltpu.VMEM((LOCAL, D), f32),
            pltpu.VMEM((D, HID), f32),
            pltpu.VMEM((HID, E), f32),
            dma((2,)), dma((6,)),
        ],
        compiler_params=pltpu.CompilerParams(vmem_limit_bytes=46 << 20),
        cost_estimate=pl.CostEstimate(
            flops=6 << 30, bytes_accessed=16 << 20, transcendentals=2 << 20
        ),
    )(hidden, turned, tallies, gain, w_in, w_out)


def body(counts, tile_mask, neighbours, peak_weight, gain, w_in, w_out):
    hidden, turned, tallies = gather_hidden(counts, tile_mask.T, neighbours, peak_weight)
    turned = pltpu.with_memory_space_constraint(turned, pltpu.HBM)
    peak_grad, gain_grad, in_grad, out_grad = tower(
        hidden, turned, tallies, gain.reshape(1, D), w_in, w_out
    )
    return (peak_grad, gain_grad.reshape(D), in_grad, out_grad)


def solution(mesh):
    cells = P(("grp", "peak"), None)
    peaks = P(None, ("grp", "peak"))
    return jax.shard_map(
        body,
        mesh=mesh,
        in_specs=(peaks, peaks, cells, cells, P(), P(), P()),
        out_specs=(cells, P(), P(), P()),
        check_vma=False,
    )
```

```python
import jax
import jax.numpy as jnp
from jax import lax
from jax.experimental import pallas as pl
from jax.experimental.pallas import tpu as pltpu
from jax.sharding import PartitionSpec as P

TILE = 128
K = 15
CELLS = 1024
D = 512
HID = 512
E = 256
LOCAL = 2048
HALF = CELLS // 2
BLOCK = 256
PIECE = BLOCK // 16
SLOT = 16

sharpness = 5.0
eps_norm = 1e-06
gelu_coef = 0.7978845608
cubic_coef = 0.044715
log2_e = 1.4426950408889634

bf16 = jnp.bfloat16
f32 = jnp.float32
i32 = jnp.int32
MESH = pl.DeviceIdType.MESH


def coordinates():
    grp = lax.axis_index("grp")
    peak = lax.axis_index("peak")
    return (grp // 2) % 4, peak // 4, (peak % 4) * 2 + grp // 8, grp % 2


def device(x, y, z, core):
    return {"grp": ((z % 2) * 4 + x) * 2 + core, "peak": y * 4 + z // 2}


def rows_of(start, size):
    return pl.ds(pl.multiple_of(start, size), size)


STEPS = sorted(
    ((dx, dy) for dx in range(4) for dy in range(4) if dx or dy),
    key=lambda step: -min(step[0], 4 - step[0]) - min(step[1], 4 - step[1]),
)


def gather_kernel(
    counts, tile_mask, neighbours, weight,
    hidden_out, turned_out, tallies_out,
    loaded, masked, turned, w_buf, mask_buf, own_lists, core_send, core_recv, plane_send,
    plane_recv, column, own_piece, lists, list_rows, counted, tallies,
    load_sem, w_sem, core_ss, core_rs, plane_ss, plane_rs, z_ss, z_rs,
    out_ss, out_rs, fwd_ss, fwd_rs, list_ss, list_rs, store_sem,
):
    x, y, z, core = coordinates()
    plane = x * 4 + y

    def send(source, target, send_sem, recv_sem, to):
        return pltpu.make_async_remote_copy(
            src_ref=source, dst_ref=target, send_sem=send_sem, recv_sem=recv_sem,
            device_id=to, device_id_type=MESH,
        )

    sibling = device(x, y, z, 1 - core)
    plane_to = [((x + dx) % 4, (y + dy) % 4) for dx, dy in STEPS]
    plane_device = [device(px, py, z, core) for px, py in plane_to]
    column_device = [device(x, y, (z + step) % 8, core) for step in (4, 3, 5, 2, 6, 1, 7)]

    barrier = pltpu.get_barrier_semaphore()
    for other in [sibling] + plane_device + column_device:
        pl.semaphore_signal(barrier, inc=1, device_id=other, device_id_type=MESH)

    def block_start(step):
        return HALF * ((core + 1 + step) % 2) + BLOCK * (step // 2)

    def load(step):
        rows = rows_of(block_start(step), BLOCK)
        return pltpu.make_async_copy(counts.at[rows], loaded.at[rows], load_sem.at[step])

    w_copy = pltpu.make_async_copy(weight, w_buf, w_sem.at[0])
    mask_copy = pltpu.make_async_copy(tile_mask, mask_buf, w_sem.at[1])
    lists_copy = pltpu.make_async_copy(neighbours, own_lists, w_sem.at[2])
    mask_copy.start()
    load(0).start()
    w_copy.start()
    lists_copy.start()
    for step in range(1, 4):
        load(step).start()

    own_slot = core * 128 + z * 16 + plane

    list_plane = [
        send(lists.at[own_slot], lists.at[own_slot], list_ss.at[i], list_rs.at[i], to)
        for i, to in enumerate(plane_device)
    ]
    list_layer = lists.at[pl.ds(core * 128 + z * 16, 16)]
    list_column = [
        send(list_layer, list_layer, list_ss.at[15 + i], list_rs.at[15 + i], to)
        for i, to in enumerate(column_device)
    ]
    list_half = lists.at[pl.ds(core * 128, 128)]
    list_core = send(list_half, list_half, list_ss.at[22], list_rs.at[22], sibling)

    def core_copy(chunk):
        return send(
            core_send.at[chunk], core_recv.at[chunk], core_ss.at[chunk], core_rs.at[chunk], sibling
        )

    def plane_copies(chunk):
        return [
            send(
                plane_send.at[chunk, px * 4 + py], plane_recv.at[chunk, i],
                plane_ss.at[chunk, i], plane_rs.at[chunk, i], plane_device[i],
            )
            for i, (px, py) in enumerate(plane_to)
        ]

    def column_copies(chunk):
        return [
            send(
                column.at[chunk, z], column.at[chunk, z],
                z_ss.at[chunk, i], z_rs.at[chunk, i], to,
            )
            for i, to in enumerate(column_device)
        ]

    def piece_rows(chunk, of):
        return rows_of(core * HALF + chunk * BLOCK + of * PIECE, PIECE)

    def keep_piece(chunk):
        return pltpu.make_async_copy(
            own_piece.at[chunk], hidden_out.at[piece_rows(chunk, plane)], store_sem.at[2 + chunk]
        )

    def out_copies(chunk):
        rows = piece_rows(chunk, plane)
        return [
            send(
                own_piece.at[chunk], hidden_out.at[rows],
                out_ss.at[chunk, i], out_rs.at[chunk, i], to,
            )
            for i, to in enumerate(plane_device)
        ]

    def fwd_copy(chunk, dx):
        start = core * HALF + chunk * BLOCK + ((x + 4 - dx) % 4) * 4 * PIECE
        rows = rows_of(start, 4 * PIECE)
        return send(
            hidden_out.at[rows], hidden_out.at[rows],
            fwd_ss.at[chunk, dx], fwd_rs.at[chunk, dx], sibling,
        )

    def peak_term(step):
        rows = rows_of(block_start(step), BLOCK)
        load(step).wait()
        keep = mask_buf[:, rows].astype(f32).T.astype(bf16)
        for tile in range(LOCAL // TILE):
            lanes = slice(tile * TILE, (tile + 1) * TILE)
            masked[rows, lanes] = loaded[rows, lanes] * jnp.broadcast_to(
                keep[:, tile : tile + 1], (BLOCK, TILE)
            )
        return jnp.dot(masked[rows, :], w_buf[...], preferred_element_type=f32)

    mask_copy.wait()
    w_copy.wait()

    def peak_chunk(chunk, carry):
        core_send[chunk] = peak_term(2 * chunk).astype(bf16)

        @pl.when(chunk == 0)
        def _():
            lists_copy.wait()
            lists[own_slot] = jnp.zeros((1, 128), i32)
            for cell in range(4):
                lists[own_slot, :, cell * SLOT : cell * SLOT + K] = own_lists[cell : cell + 1, :]
            pl.semaphore_wait(barrier, 23)

        core_copy(chunk).start()

        @pl.when(chunk == 0)
        def _():
            for copy in list_plane:
                copy.start()

        term = peak_term(2 * chunk + 1)
        core_copy(chunk).wait()
        plane_send[chunk] = (term + core_recv[chunk].astype(f32)).astype(bf16).reshape(
            16, PIECE, D
        )
        for copy in plane_copies(chunk):
            copy.start()
        return carry

    lax.fori_loop(0, 2, peak_chunk, 0)
    for copy in list_plane:
        copy.wait()
    for copy in list_column:
        copy.start()

    def turn(step, carry):
        rows = rows_of(step * 128, 128)
        for tile in range(LOCAL // TILE):
            lanes = slice(tile * TILE, (tile + 1) * TILE)
            turned[lanes, rows] = masked[rows, lanes].T
        return carry

    def add_plane(chunk):
        total = plane_send[chunk, plane].astype(f32)
        for i, copy in enumerate(plane_copies(chunk)):
            copy.wait_recv()
            total += plane_recv[chunk, i].astype(f32)
        column[chunk, z] = total.astype(bf16)
        for copy in column_copies(chunk):
            copy.start()

    lax.fori_loop(0, 3, turn, 0)
    add_plane(0)
    lax.fori_loop(3, 6, turn, 0)
    add_plane(1)
    for copy in list_column:
        copy.wait()
    list_core.start()
    lax.fori_loop(6, 8, turn, 0)
    turned_store = pltpu.make_async_copy(turned, turned_out, store_sem.at[0])
    turned_store.start()
    list_core.wait()

    by_slot = lists[:, 0, :].astype(f32).T
    place = lax.broadcasted_iota(i32, (CELLS // 4, 1), 0)
    at_core, at_z, at_x, at_y = place // 128, (place // 16) % 8, (place // 4) % 4, place % 4
    holder = (((at_z % 2) * 4 + at_x) * 2 + at_core) * 16 + at_y * 4 + at_z // 2
    cells = lax.broadcasted_iota(i32, (CELLS // 4, CELLS), 1)
    gathered = jnp.zeros((2 * SLOT, CELLS), f32)
    for cell in range(4):
        chosen = (holder * 4 + cell == cells).astype(f32).astype(bf16)
        entry = by_slot[cell * SLOT : (cell + 1) * SLOT, :]
        high = jnp.floor(entry * (1.0 / 32.0))
        low = entry - 32.0 * high
        gathered += jnp.dot(
            jnp.concatenate([high, low], axis=0).astype(bf16), chosen, preferred_element_type=f32
        )
    list_rows[...] = gathered

    def count(part, carry):
        lanes = rows_of(part * 128, 128)
        ids = lax.broadcasted_iota(i32, (32, 128), 0).astype(f32)
        low_is, high = [], []
        for slot in range(K):
            entry = jnp.broadcast_to(list_rows[SLOT + slot : SLOT + slot + 1, lanes], (32, 128))
            low_is.append(jnp.where(entry == ids, 1.0, 0.0).astype(bf16))
            entry = jnp.broadcast_to(list_rows[slot : slot + 1, lanes], (32, 128))
            high.append(entry.astype(bf16))
        none = jnp.zeros((32, 128), bf16)

        def count_rows(step, carry):
            this = jnp.full((32, 128), step.astype(f32), f32).astype(bf16)
            total = none
            for slot in range(K):
                total += jnp.where(high[slot] == this, low_is[slot], none)
            counted[rows_of(step * 32, 32), lanes] = total
            return carry

        return lax.fori_loop(0, CELLS // 32, count_rows, carry, unroll=4)

    def add_column(chunk):
        for copy in column_copies(chunk):
            copy.wait_recv()
        whole = column[chunk, 0].astype(f32)
        for step in range(1, 8):
            whole += column[chunk, step].astype(f32)
        own_piece[chunk] = whole.astype(bf16)
        for copy in out_copies(chunk):
            copy.start()
        keep_piece(chunk).start()

    def pass_on(chunk):
        arrived = out_copies(chunk)
        keep_piece(chunk).wait()
        for dx in range(4):
            for i, step in enumerate(STEPS):
                if step[0] == dx:
                    arrived[i].wait_recv()
            fwd_copy(chunk, dx).start()

    lax.fori_loop(0, 3, count, 0)
    add_column(0)
    lax.fori_loop(3, 8, count, 0)
    add_column(1)

    def both(step, carry):
        rows = rows_of(step * 128, 128)
        for part in range(CELLS // 128):
            lanes = slice(part * 128, (part + 1) * 128)
            tallies[rows, lanes] = counted[rows, lanes] + counted[lanes, rows].T
        return carry

    lax.fori_loop(0, CELLS // 128, both, 0)
    tallies_store = pltpu.make_async_copy(tallies, tallies_out, store_sem.at[1])
    tallies_store.start()
    pass_on(0)
    pass_on(1)
    for chunk in range(2):
        for copy in plane_copies(chunk) + column_copies(chunk) + out_copies(chunk):
            copy.wait_send()
    for chunk in range(2):
        for dx in range(4):
            fwd_copy(chunk, dx).wait()
    turned_store.wait()
    tallies_store.wait()


MASK_T = True


def gather_hidden(counts, tile_mask, neighbours, weight):
    hbm = pl.BlockSpec(memory_space=pltpu.HBM)
    dma = pltpu.SemaphoreType.DMA
    return pl.pallas_call(
        gather_kernel,
        name="gather_hidden",
        out_shape=(
            jax.ShapeDtypeStruct((CELLS, D), bf16),
            jax.ShapeDtypeStruct((LOCAL, CELLS), bf16),
            jax.ShapeDtypeStruct((CELLS, CELLS), bf16),
        ),
        in_specs=[hbm, hbm, hbm, hbm],
        out_specs=(pl.BlockSpec(memory_space=pl.ANY), hbm, hbm),
        scratch_shapes=[
            pltpu.VMEM((CELLS, LOCAL), bf16),
            pltpu.VMEM((CELLS, LOCAL), bf16),
            pltpu.VMEM((LOCAL, CELLS), bf16),
            pltpu.VMEM((LOCAL, D), bf16),
            pltpu.VMEM((LOCAL // TILE, CELLS), i32),
            pltpu.VMEM((4, K), i32),
            pltpu.VMEM((2, BLOCK, D), bf16),
            pltpu.VMEM((2, BLOCK, D), bf16),
            pltpu.VMEM((2, 16, PIECE, D), bf16),
            pltpu.VMEM((2, 15, PIECE, D), bf16),
            pltpu.VMEM((2, 8, PIECE, D), bf16),
            pltpu.VMEM((2, PIECE, D), bf16),
            pltpu.VMEM((CELLS // 4, 1, 128), i32),
            pltpu.VMEM((2 * SLOT, CELLS), f32),
            pltpu.VMEM((CELLS, CELLS), bf16),
            pltpu.VMEM((CELLS, CELLS), bf16),
            dma((4,)), dma((3,)), dma((2,)), dma((2,)), dma((2, 15)), dma((2, 15)),
            dma((2, 7)), dma((2, 7)), dma((2, 15)), dma((2, 15)), dma((2, 4)), dma((2, 4)),
            dma((23,)), dma((23,)), dma((4,)),
        ],
        compiler_params=pltpu.CompilerParams(
            collective_id=0, has_side_effects=True, vmem_limit_bytes=48 << 20
        ),
        cost_estimate=pl.CostEstimate(
            flops=2 * CELLS * LOCAL * D, bytes_accessed=16 << 20, transcendentals=0
        ),
    )(*(pltpu.with_memory_space_constraint(v, pltpu.HBM) for v in (counts, tile_mask, neighbours, weight)))


def across(left, right):
    return lax.dot_general(left, right, (((1,), (1,)), ((), ())), preferred_element_type=f32)


def collapsed(left, right):
    return lax.dot_general(left, right, (((0,), (0,)), ((), ())), preferred_element_type=f32)


def tower_kernel(
    hidden, turned, tallies, gain, w_in, w_out,
    peak_grad, gain_grad, in_grad, out_grad,
    turned_buf, tallies_buf, rounded, slope, activ, unit, length, scale, codes, expo, inverse,
    dproj, dpre, dhidden, peak_buf, in_buf, out_buf, load_sem, store_sem,
):
    tallies_copy = pltpu.make_async_copy(tallies, tallies_buf, load_sem.at[0])
    tallies_copy.start()
    turned_copy = pltpu.make_async_copy(turned, turned_buf, load_sem.at[1])
    turned_copy.start()

    step_rows = 512

    def forward(step, carry):
        rows = rows_of(step * step_rows, step_rows)
        h = hidden[rows, :].astype(f32)
        s = lax.rsqrt(jnp.mean(h * h, axis=1, keepdims=True) + eps_norm)
        scale[rows, :] = s
        r = (h * s * gain[...]).astype(bf16)
        rounded[rows, :] = r
        v = jnp.dot(r, w_in[...], preferred_element_type=f32)
        square = v * v
        t = jnp.tanh(v * (gelu_coef + (gelu_coef * cubic_coef) * square))
        half_v = 0.5 * v
        a = (half_v + half_v * t).astype(bf16)
        activ[rows, :] = a
        slope[rows, :] = (0.5 + 0.5 * t) + half_v * (1.0 - t * t) * (
            gelu_coef + (3.0 * gelu_coef * cubic_coef) * square
        )
        p = jnp.dot(a, w_out[...], preferred_element_type=f32)
        n = lax.rsqrt(jnp.sum(p * p, axis=1, keepdims=True) + eps_norm)
        length[rows, :] = n
        u = p * n
        unit[rows, :] = u
        codes[rows, :] = u.astype(bf16)
        return carry

    lax.fori_loop(0, CELLS // step_rows, forward, 0)

    expo[...] = jnp.exp2(across(codes[...], codes[...]) * (sharpness * log2_e))
    diagonal = lax.broadcasted_iota(i32, (128, 128), 0) == lax.broadcasted_iota(i32, (128, 128), 1)
    for part in range(CELLS // 128):
        block = slice(part * 128, (part + 1) * 128)
        expo[block, block] = jnp.where(diagonal, 0.0, expo[block, block])
    e = expo[...]
    inverse[...] = 1.0 / jnp.sum(e, axis=1, keepdims=True)
    column_inverse = 1.0 / jnp.sum(e, axis=0, keepdims=True)
    tallies_copy.wait()

    both = expo[...] * (inverse[...] + column_inverse)
    both = (both - tallies_buf[...].astype(f32) * (1.0 / K)).astype(bf16)
    dcodes = jnp.dot(both, codes[...], preferred_element_type=f32) * sharpness
    u = unit[...]
    dp = (length[...] * (dcodes - u * jnp.sum(u * dcodes, axis=1, keepdims=True))).astype(bf16)
    dproj[...] = dp
    dv = (across(dp, w_out[...]) * slope[...]).astype(bf16)
    dpre[...] = dv
    dround = across(dv, w_in[...])
    normed = hidden[...].astype(f32) * scale[...]
    dnorm = dround * gain[...]
    dhidden[...] = (
        scale[...] * (dnorm - normed * jnp.mean(dnorm * normed, axis=1, keepdims=True))
    ).astype(bf16)
    gain_grad[...] = jnp.sum(dround * normed, axis=0, keepdims=True)

    in_buf[...] = collapsed(rounded[...], dpre[...])
    in_store = pltpu.make_async_copy(in_buf, in_grad, store_sem.at[4])
    in_store.start()
    out_buf[...] = collapsed(activ[...], dproj[...])
    out_store = pltpu.make_async_copy(out_buf, out_grad, store_sem.at[5])
    out_store.start()
    turned_copy.wait()

    def store(step):
        rows = rows_of(step * step_rows, step_rows)
        return pltpu.make_async_copy(peak_buf.at[rows], peak_grad.at[rows], store_sem.at[step])

    def peak(step, carry):
        rows = rows_of(step * step_rows, step_rows)
        peak_buf[rows, :] = jnp.dot(turned_buf[rows, :], dhidden[...], preferred_element_type=f32)
        store(step).start()
        return carry

    lax.fori_loop(0, LOCAL // step_rows, peak, 0)
    in_store.wait()
    out_store.wait()
    def stored(step, carry):
        store(step).wait()
        return carry

    lax.fori_loop(0, LOCAL // step_rows, stored, 0)


def tower(hidden, turned, tallies, gain, w_in, w_out):
    any_space = pl.BlockSpec(memory_space=pl.ANY)
    vmem = pl.BlockSpec(memory_space=pltpu.VMEM)
    dma = pltpu.SemaphoreType.DMA
    return pl.pallas_call(
        tower_kernel,
        name="tower",
        out_shape=(
            jax.ShapeDtypeStruct((LOCAL, D), f32),
            jax.ShapeDtypeStruct((1, D), f32),
            jax.ShapeDtypeStruct((D, HID), f32),
            jax.ShapeDtypeStruct((HID, E), f32),
        ),
        in_specs=[vmem, any_space, any_space, vmem, vmem, vmem],
        out_specs=(any_space, vmem, any_space, any_space),
        scratch_shapes=[
            pltpu.VMEM((LOCAL, CELLS), bf16),
            pltpu.VMEM((CELLS, CELLS), bf16),
            pltpu.VMEM((CELLS, D), bf16),
            pltpu.VMEM((CELLS, HID), f32),
            pltpu.VMEM((CELLS, HID), bf16),
            pltpu.VMEM((CELLS, E), f32),
            pltpu.VMEM((CELLS, 1), f32),
            pltpu.VMEM((CELLS, 1), f32),
            pltpu.VMEM((CELLS, E), bf16),
            pltpu.VMEM((CELLS, CELLS), f32),
            pltpu.VMEM((CELLS, 1), f32),
            pltpu.VMEM((CELLS, E), bf16),
            pltpu.VMEM((CELLS, HID), bf16),
            pltpu.VMEM((CELLS, D), bf16),
            pltpu.VMEM((LOCAL, D), f32),
            pltpu.VMEM((D, HID), f32),
            pltpu.VMEM((HID, E), f32),
            dma((2,)), dma((6,)),
        ],
        compiler_params=pltpu.CompilerParams(vmem_limit_bytes=46 << 20),
        cost_estimate=pl.CostEstimate(
            flops=6 << 30, bytes_accessed=16 << 20, transcendentals=2 << 20
        ),
    )(hidden, turned, tallies, gain, w_in, w_out)


def body(counts, tile_mask, neighbours, peak_weight, gain, w_in, w_out):
    hidden, turned, tallies = gather_hidden(counts, tile_mask.T, neighbours, peak_weight)
    turned = pltpu.with_memory_space_constraint(turned, pltpu.HBM)
    peak_grad, gain_grad, in_grad, out_grad = tower(
        hidden, turned, tallies, gain.reshape(1, D), w_in, w_out
    )
    return (peak_grad, gain_grad.reshape(D), in_grad, out_grad)


def solution(mesh):
    cells = P(("grp", "peak"), None)
    peaks = P(None, ("grp", "peak"))
    return jax.shard_map(
        body,
        mesh=mesh,
        in_specs=(peaks, peaks, cells, cells, P(), P(), P()),
        out_specs=(cells, P(), P(), P()),
        check_vma=False,
    )
```
